256 devices in a mesh: seq: 32 (over z, y_lo, core), head: 8 (over y_hi, x).
Axes of the slice: x: 4, y: 4 (y_hi: 2, y_lo: 2; y = y_hi * 2 + y_lo), z: 8, core: 2. Of those that a mesh axis runs over, the one named last changes fastest.
Arguments:
- normed_layer_input: bfloat16 [8192, 8192], P('seq', 'head'), may hold values from -6 to 6
- query_projection_input: bfloat16 [8192, 8192], P('seq', 'head'), may hold values from -9 to 9, as said below
- key_projection_input: bfloat16 [8192, 1024], P('seq', 'head'), may hold values from -9 to 9, as said below
- value_projection_input: bfloat16 [8192, 1024], P('seq', 'head'), may hold values from -6 to 6
- output_gradient: bfloat16 [8192, 8192], P('seq', 'head'), may hold values from -12 to 12
- adapter_down_weight: bfloat16 [3, 8, 8192], P(None, None, 'head'), may hold values from -0.0007324219 to 0.0007324219
- adapter_up_query: bfloat16 [8, 8192], P(None, 'head'), may hold values from -0.0007324219 to 0.0007324219
- adapter_up_kv: bfloat16 [2, 8, 1024], P(None, None, 'head'), may hold values from -0.001953125 to 0.001953125
Outputs:
- query_projection_gradient: bfloat16 [8192, 8192], P('seq', 'head')
- key_projection_gradient: bfloat16 [8192, 1024], P('seq', 'head')
- value_projection_gradient: bfloat16 [8192, 1024], P('seq', 'head')
- adapter_down_gradient: float32 [3, 8, 8192], P(None, None, 'head')
- adapter_up_query_gradient: float32 [8, 8192], P(None, 'head')
- adapter_up_kv_gradient: float32 [2, 8, 1024], P(None, None, 'head')
The draws below stay inside these ranges and needn't reach their ends.
Inputs may be any that keep to these rules, and one draw needn't show every extreme that they name: `query_projection_input`: real values. `key_projection_input`: real values.
All inputs are finite; a program needn't handle non-finite values.
Results may differ from the reference program's by a relative error of at most 0.029.
Values may be sent and summed in bfloat16 or wider, within the bound.
A program may use at most 64 MiB of HBM per device.

```python
import jax
import jax.numpy as jnp
from jax import lax

MODEL_WIDTH = 8192
HEAD_SIZE = 128
QUERY_PER_KV = 8
ADAPTER_RANK = 8
SEQUENCE_TOKENS = 8192
GROUP = 2048
HALF = 1024
KV_HEADS = 8
QUERY_HEADS = 64


def drawn_pair(base_key):
    row_count = SEQUENCE_TOKENS
    query_cols = QUERY_HEADS * HEAD_SIZE
    key_cols = KV_HEADS * HEAD_SIZE
    first_key = jax.random.fold_in(base_key, 101)
    second_key = jax.random.fold_in(base_key, 202)
    query_out = 1.5 * jnp.clip(jax.random.normal(first_key, (row_count, query_cols), jnp.float32), -3.0, 3.0)
    key_out = 1.5 * jnp.clip(jax.random.normal(second_key, (row_count, key_cols), jnp.float32), -3.0, 3.0)
    return (query_out.astype(jnp.bfloat16), key_out.astype(jnp.bfloat16))


def draw_query_projection_input(key, part):
    return drawn_pair(key)[0]


def draw_key_projection_input(key, part):
    return drawn_pair(key)[1]


def block_levels(key, extent, cuts, least, top_value):
    def one(position, parts):
        heights = jax.random.uniform(jax.random.fold_in(jax.random.fold_in(key, 6), position), (parts,), jnp.float32, least / len(cuts), top_value / len(cuts))
        return jnp.repeat(jnp.exp(heights), extent[position] // parts).reshape((-1,) + (1,) * (len(extent) - position - 1))

    loudness = one(*cuts[0])
    for cut in cuts[1:]:
        loudness = loudness * one(*cut)
    return loudness


def centred(stream_key, extent, spread, most, shards=(), held_as=jnp.bfloat16):
    values = spread * jax.random.normal(stream_key, extent, jnp.float32)
    if shards:
        values = values * block_levels(stream_key, extent, shards, -0.22, 0.18)
    return jnp.clip(values, -most, most).astype(held_as)


def setup_inputs(seed: int = 0) -> dict:
    seeds = jax.random.split(jax.random.key(seed), 9)
    return {
        "normed_layer_input": centred(seeds[0], (SEQUENCE_TOKENS, MODEL_WIDTH), 1.0, 6.0, ((0, 32), (1, 8))),
        "query_projection_input": draw_query_projection_input(jax.random.fold_in(seeds[8], 71), 0),
        "key_projection_input": draw_key_projection_input(jax.random.fold_in(seeds[8], 71), 0),
        "value_projection_input": centred(seeds[3], (SEQUENCE_TOKENS, KV_HEADS * HEAD_SIZE), 1.0, 6.0, ((0, 32), (1, 8))),
        "output_gradient": centred(seeds[4], (SEQUENCE_TOKENS, QUERY_HEADS * HEAD_SIZE), 2.0, 12.0, ((0, 32), (1, 8))),
        "adapter_down_weight": centred(seeds[5], (3, ADAPTER_RANK, MODEL_WIDTH), (MODEL_WIDTH * SEQUENCE_TOKENS) ** -0.5, 0.0007324219, ((2, 8),)),
        "adapter_up_query": centred(seeds[6], (ADAPTER_RANK, QUERY_HEADS * HEAD_SIZE), (QUERY_HEADS * HEAD_SIZE * SEQUENCE_TOKENS) ** -0.5, 0.0007324219, ((1, 8),)),
        "adapter_up_kv": centred(seeds[7], (2, ADAPTER_RANK, KV_HEADS * HEAD_SIZE), (KV_HEADS * HEAD_SIZE * SEQUENCE_TOKENS) ** -0.5, 0.001953125, ((2, 8),)),
    }


position_scale = 0.04096


def rope_tables(positions, feature_count):
    half_width = feature_count // 2
    frequency = position_scale * 10000.0 ** (-2.0 * jnp.arange(half_width, dtype=jnp.float32) / feature_count)
    angles = positions.astype(jnp.float32)[:, None] * frequency[None, :]
    return jnp.cos(angles)[:, None, :], jnp.sin(angles)[:, None, :]


def rotate(vectors, cosine_table, sine_table):
    half_width = vectors.shape[-1] // 2
    low_half = vectors[..., :half_width]
    high_half = vectors[..., half_width:]
    return jnp.concatenate([low_half * cosine_table - high_half * sine_table, high_half * cosine_table + low_half * sine_table], axis=-1)


def unrotate(gradient, cosine_table, sine_table):
    half_width = gradient.shape[-1] // 2
    low_half = gradient[..., :half_width]
    high_half = gradient[..., half_width:]
    return jnp.concatenate([low_half * cosine_table + high_half * sine_table, high_half * cosine_table - low_half * sine_table], axis=-1)


def group_grads(operands):
    query_rot, key_rot, value_blk, grad_blk = operands
    length = query_rot.shape[0]
    score_scale = HEAD_SIZE ** -0.5
    scores = jnp.dot(query_rot, key_rot.T, preferred_element_type=jnp.float32) * score_scale
    allowed = jnp.arange(length, dtype=jnp.int32)[:, None] >= jnp.arange(length, dtype=jnp.int32)[None, :]
    masked = jnp.where(allowed, scores, -jnp.inf)
    row_top = jnp.max(masked, axis=1, keepdims=True)
    log_total = row_top + jnp.log(jnp.sum(jnp.exp(masked - row_top), axis=1, keepdims=True))
    weights = jnp.where(allowed, jnp.exp(scores - log_total), 0.0)
    prob_bf16 = weights.astype(jnp.bfloat16)
    attn_out = jnp.dot(prob_bf16, value_blk, preferred_element_type=jnp.float32).astype(jnp.bfloat16)
    row_delta = jnp.sum(attn_out.astype(jnp.float32) * grad_blk.astype(jnp.float32), axis=1, keepdims=True)
    prob_grad = jnp.dot(grad_blk, value_blk.T, preferred_element_type=jnp.float32)
    dscore = (weights * (prob_grad - row_delta)).astype(jnp.bfloat16)
    query_part = jnp.dot(dscore, key_rot, preferred_element_type=jnp.float32) * score_scale
    key_part = jnp.dot(dscore.T, query_rot, preferred_element_type=jnp.float32) * score_scale
    value_part = jnp.dot(prob_bf16.T, grad_blk, preferred_element_type=jnp.float32)
    return query_part, key_part, value_part


def reference(normed_layer_input, query_projection_input, key_projection_input, value_projection_input, output_gradient, adapter_down_weight, adapter_up_query, adapter_up_kv):
    positions = jnp.arange(SEQUENCE_TOKENS, dtype=jnp.int32)
    cosine_table, sine_table = rope_tables(positions, HEAD_SIZE)
    query_rot = rotate(query_projection_input.astype(jnp.float32).reshape(SEQUENCE_TOKENS, QUERY_HEADS, HEAD_SIZE), cosine_table, sine_table).astype(jnp.bfloat16)
    key_rot = rotate(key_projection_input.astype(jnp.float32).reshape(SEQUENCE_TOKENS, KV_HEADS, HEAD_SIZE), cosine_table, sine_table).astype(jnp.bfloat16)
    value_heads = value_projection_input.reshape(SEQUENCE_TOKENS, KV_HEADS, HEAD_SIZE)
    grad_heads = output_gradient.reshape(SEQUENCE_TOKENS, QUERY_HEADS, HEAD_SIZE)
    query_list = []
    key_list = []
    value_list = []
    for kv_index in range(KV_HEADS):
        moved = kv_index >= KV_HEADS // 2
        key_member = key_rot[:, kv_index]
        value_member = value_heads[:, kv_index]
        if moved:
            key_member = jnp.roll(key_member, -HALF, axis=0)
            value_member = jnp.roll(value_member, -HALF, axis=0)
        key_total = jnp.zeros((SEQUENCE_TOKENS, HEAD_SIZE), jnp.float32)
        value_total = jnp.zeros((SEQUENCE_TOKENS, HEAD_SIZE), jnp.float32)
        for query_index in range(kv_index * QUERY_PER_KV, (kv_index + 1) * QUERY_PER_KV):
            query_member = query_rot[:, query_index]
            grad_member = grad_heads[:, query_index]
            if moved:
                query_member = jnp.roll(query_member, -HALF, axis=0)
                grad_member = jnp.roll(grad_member, -HALF, axis=0)
            grouped = tuple(member.reshape(4, GROUP, HEAD_SIZE) for member in [query_member, key_member, value_member, grad_member])
            results = lax.map(group_grads, grouped)
            query_part = results[0].reshape(SEQUENCE_TOKENS, HEAD_SIZE)
            if moved:
                query_part = jnp.roll(query_part, HALF, axis=0)
            query_list.append(query_part)
            key_total = key_total + results[1].reshape(SEQUENCE_TOKENS, HEAD_SIZE)
            value_total = value_total + results[2].reshape(SEQUENCE_TOKENS, HEAD_SIZE)
        if moved:
            key_total = jnp.roll(key_total, HALF, axis=0)
            value_total = jnp.roll(value_total, HALF, axis=0)
        key_list.append(key_total)
        value_list.append(value_total)
    query_rot_grad = jnp.stack(query_list, axis=1)
    key_rot_grad = jnp.stack(key_list, axis=1)
    query_projection_gradient = unrotate(query_rot_grad, cosine_table, sine_table).astype(jnp.bfloat16).reshape(SEQUENCE_TOKENS, QUERY_HEADS * HEAD_SIZE)
    key_projection_gradient = unrotate(key_rot_grad, cosine_table, sine_table).astype(jnp.bfloat16).reshape(SEQUENCE_TOKENS, KV_HEADS * HEAD_SIZE)
    value_projection_gradient = jnp.stack(value_list, axis=1).astype(jnp.bfloat16).reshape(SEQUENCE_TOKENS, KV_HEADS * HEAD_SIZE)
    down_activation = jnp.dot(normed_layer_input, adapter_down_weight.reshape(3 * ADAPTER_RANK, MODEL_WIDTH).T, preferred_element_type=jnp.float32).astype(jnp.bfloat16).reshape(SEQUENCE_TOKENS, 3, ADAPTER_RANK)
    back_query = jnp.dot(query_projection_gradient, adapter_up_query.T, preferred_element_type=jnp.float32)
    back_key = jnp.dot(key_projection_gradient, adapter_up_kv[0].T, preferred_element_type=jnp.float32)
    back_value = jnp.dot(value_projection_gradient, adapter_up_kv[1].T, preferred_element_type=jnp.float32)
    backward_activation = jnp.stack([back_query, back_key, back_value], axis=1).astype(jnp.bfloat16)
    kv_pile = jnp.stack([key_projection_gradient, value_projection_gradient])
    adapter_up_query_gradient = 2.0 * jnp.einsum("yj,yq->jq", down_activation[:, 0].astype(jnp.float32), query_projection_gradient.astype(jnp.float32), precision=lax.Precision.HIGHEST)
    adapter_up_kv_gradient = 2.0 * jnp.einsum("yij,iyq->ijq", down_activation[:, 1:].astype(jnp.float32), kv_pile.astype(jnp.float32), precision=lax.Precision.HIGHEST)
    adapter_down_gradient = 2.0 * jnp.einsum("yhu,ym->hum", backward_activation.astype(jnp.float32), normed_layer_input.astype(jnp.float32), precision=lax.Precision.HIGHEST)
    return query_projection_gradient, key_projection_gradient, value_projection_gradient, adapter_down_gradient, adapter_up_query_gradient, adapter_up_kv_gradient
```

```python
import functools

import jax
import jax.numpy as jnp
from jax import lax
from jax.experimental import pallas as pl
from jax.experimental.pallas import tpu as pltpu
from jax.sharding import PartitionSpec as P

HEAD_SIZE = 128
POSITION_SCALE = 0.04096
LOG2E = 1.4426950408889634
MESH = pl.DeviceIdType.MESH
F32 = jnp.float32
BF16 = jnp.bfloat16
GROUP = 8
QUAD = 4
NT = (((1,), (1,)), ((), ()))


def dot(a, b):
    return jnp.dot(a, b, preferred_element_type=F32)


def dot_nt(a, b):
    return lax.dot_general(a, b, NT, preferred_element_type=F32)


def kernel(
    seq_count,
    head_count,
    q_ref,
    k_ref,
    v_ref,
    do_ref,
    x_ref,
    wd_ref,
    uq_ref,
    ukv_ref,
    dq_ref,
    dk_ref,
    dv_ref,
    gd_ref,
    guq_ref,
    gukv_ref,
    kv_all,
    kt_all,
    q_rot,
    do_hm,
    e_buf,
    dp_buf,
    m_blk,
    m_run,
    l_run,
    d_run,
    p_t,
    ds_t,
    dq_t,
    acc,
    part_out,
    pair_in,
    chip_in,
    down_out,
    down_in,
    back_out,
    back_in,
    rs1_out,
    rs1_in,
    z1_out,
    z1_in,
    g1_out,
    g1_in,
    rs2_out,
    rs2_in,
    z2_out,
    z2_in,
    g2_out,
    g2_in,
    kv_s,
    kv_r,
    fw_s,
    part_s,
    pair_r,
    chip_r,
    down_s,
    down_r,
    back_s,
    back_r,
    rs1_s,
    rs1_r,
    z1_s,
    z1_r,
    g1_s,
    g1_r,
    rs2_s,
    rs2_r,
    z2_s,
    z2_r,
    g2_s,
    g2_r,
):
    rows = k_ref.shape[0]
    heads = q_ref.shape[1] // HEAD_SIZE
    width = heads * HEAD_SIZE
    score_scale = HEAD_SIZE ** -0.5
    s = lax.axis_index("seq")
    h = lax.axis_index("head")
    shift = jnp.where(h >= head_count // 2, GROUP // 2, 0)
    place = (s + seq_count - shift) % GROUP
    chip = place // 2
    core = place % 2
    unit = s % QUAD
    z = s // QUAD
    z_count = seq_count // QUAD

    def at_place(q):
        return ((s + seq_count - place + q) % seq_count, h)

    partner = at_place(place + 1 - 2 * core)

    def at_head(i):
        return (s, i)

    def at_unit(i):
        return (z * QUAD + i, h)

    def at_z(i):
        return (i * QUAD + unit, h)

    def rc(src, dst, ss, rs, dev):
        return pltpu.make_async_remote_copy(
            src_ref=src, dst_ref=dst, send_sem=ss, recv_sem=rs, device_id=dev, device_id_type=MESH
        )

    barrier = pltpu.get_barrier_semaphore()

    def greet(i, carry):
        pl.semaphore_signal(barrier, inc=1, device_id=at_place((place + i) % GROUP), device_id_type=MESH)
        pl.semaphore_signal(barrier, inc=1, device_id=at_head((h + i) % head_count), device_id_type=MESH)
        pl.semaphore_signal(barrier, inc=1, device_id=at_z((z + i) % z_count), device_id_type=MESH)
        return carry

    lax.fori_loop(1, 8, greet, 0)

    half = HEAD_SIZE // 2
    lane = lax.broadcasted_iota(jnp.int32, (1, HEAD_SIZE), 1)
    feature = (lane % half).astype(F32)
    frequency = POSITION_SCALE * jnp.exp(feature * (-2.0 / HEAD_SIZE * 9.210340371976184))
    position = (s * rows + lax.broadcasted_iota(jnp.int32, (rows, 1), 0)).astype(F32)
    angle = position * frequency
    cosine = jnp.cos(angle)
    sine = jnp.where(lane < half, -1.0, 1.0) * jnp.sin(angle)

    def rotate(x):
        return x * cosine + pltpu.roll(x, half, 1) * sine

    def unrotate(x):
        return x * cosine - pltpu.roll(x, half, 1) * sine

    kv_all[place, 0] = rotate(k_ref[...].astype(F32)).astype(BF16)
    kv_all[place, 1] = v_ref[...]
    down_out[...] = dot_nt(wd_ref[...], x_ref[...]).astype(BF16)
    down_in[h] = down_out[...]
    for i in range(heads):
        cols = slice(i * HEAD_SIZE, (i + 1) * HEAD_SIZE)
        q_rot[i * rows : (i + 1) * rows, :] = rotate(q_ref[:, cols].astype(F32)).astype(BF16)
        do_hm[i * rows : (i + 1) * rows, :] = do_ref[:, cols]

    pl.semaphore_wait(barrier, 21)

    def kv_copy(q):
        return rc(kv_all.at[place], kv_all.at[place], kv_s.at[q], kv_r.at[place], at_place(q))

    @pl.when(core == 0)
    def _():
        kv_copy(place + 1).start()

    def kv_start(i, carry):
        kv_copy(2 * i + core).start()
        return carry

    lax.fori_loop(chip + 1, QUAD, kv_start, 0)

    def head_loop(fn):
        lax.fori_loop(1, head_count, lambda i, c: (fn((h + i) % head_count), c)[1], 0)

    head_loop(lambda i: rc(down_out, down_in.at[h], down_s.at[i], down_r.at[h], at_head(i)).start())

    def forward_block(j, masked):
        keys = kv_all[j, 0]
        values = kv_all[j, 1]
        kt_all[j] = keys.T
        for i in range(heads):
            span = slice(i * rows, (i + 1) * rows)
            st = dot_nt(keys, q_rot[span, :])
            dp = dot_nt(values, do_hm[span, :])
            if masked:
                key_pos = lax.broadcasted_iota(jnp.int32, (rows, rows), 0)
                query_pos = lax.broadcasted_iota(jnp.int32, (rows, rows), 1)
                st = jnp.where(key_pos <= query_pos, st, -1e30)
                top = jnp.max(st, axis=0, keepdims=True)
                e = jnp.exp2((st - top) * (score_scale * LOG2E))
                l_run[i] = jnp.sum(e, axis=0, keepdims=True)
                d_run[i] = jnp.sum(e * dp, axis=0, keepdims=True)
            else:
                old = m_run[i]
                top = jnp.maximum(old, jnp.max(st, axis=0, keepdims=True))
                e = jnp.exp2((st - top) * (score_scale * LOG2E))
                fix = jnp.exp2((old - top) * (score_scale * LOG2E))
                l_run[i] = l_run[i] * fix + jnp.sum(e, axis=0, keepdims=True)
                d_run[i] = d_run[i] * fix + jnp.sum(e * dp, axis=0, keepdims=True)
            m_run[i] = top
            m_blk[j, i] = top
            e_buf[j, :, span] = e
            dp_buf[j, :, span] = dp

    forward_block(place, True)

    def forward_step(u, carry):
        par = u % 2
        j = 2 * (chip - u // 2) + core + par * (1 - 2 * core)
        rc(kv_all.at[j], kv_all.at[j], kv_s.at[j], kv_r.at[j], partner).wait_recv()

        @pl.when(par == 0)
        def _():
            rc(kv_all.at[j], kv_all.at[j], fw_s.at[j], kv_r.at[j], partner).start()

        forward_block(j, False)
        return carry

    lax.fori_loop(2 - core, 2 * chip + 2, forward_step, 0)

    for i in range(heads):
        inv = 1.0 / l_run[i]
        l_run[i] = inv
        d_run[i] = d_run[i] * inv

    dq_t[...] = jnp.zeros_like(dq_t)

    def backward_block(j):
        for i in range(heads):
            span = slice(i * rows, (i + 1) * rows)
            scale = jnp.exp2((m_blk[j, i] - m_run[i]) * (score_scale * LOG2E)) * l_run[i]
            prob = e_buf[j, :, span] * scale
            p_t[:, span] = prob.astype(BF16)
            ds_t[:, span] = (prob * (dp_buf[j, :, span] - d_run[i])).astype(BF16)
        dq_t[...] += dot(kt_all[j], ds_t[...])
        return dot(ds_t[...], q_rot[...]), dot(p_t[...], do_hm[...])

    def part_copy_pair(j):
        return rc(part_out.at[j], pair_in.at[j], part_s.at[j], pair_r.at[j], partner)

    def part_copy_chip(j):
        return rc(part_out.at[j], chip_in.at[chip], part_s.at[j], chip_r.at[chip], at_place(j))

    def backward_step(w, carry):
        par = w % 2
        j = 2 * (w // 2) + (1 - core) + par * (2 * core - 1)
        key_part, value_part = backward_block(j)

        @pl.when(par == 0)
        def _():
            part_out[j, 0] = key_part.astype(BF16)
            part_out[j, 1] = value_part.astype(BF16)
            part_copy_pair(j).start()

        @pl.when(par == 1)
        def _():
            part_copy_pair(j).wait_recv()
            part_out[j, 0] = (key_part + pair_in[j, 0].astype(F32)).astype(BF16)
            part_out[j, 1] = (value_part + pair_in[j, 1].astype(F32)).astype(BF16)
            part_copy_chip(j).start()

        return carry

    lax.fori_loop(0, place, backward_step, 0)
    key_part, value_part = backward_block(place)
    acc[0] = key_part
    acc[1] = value_part

    back = jnp.zeros((8, rows), F32)
    for i in range(heads):
        span = slice(i * rows, (i + 1) * rows)
        cols = slice(i * HEAD_SIZE, (i + 1) * HEAD_SIZE)
        grad = unrotate(dq_t[:, span].T * score_scale).astype(BF16)
        dq_ref[:, cols] = grad
        back += dot_nt(uq_ref[:, cols], grad)
    back_out[0:8, :] = back.astype(BF16)

    @pl.when(core == 0)
    def _():
        rc(part_out.at[place], pair_in.at[place], part_s.at[place], pair_r.at[place], partner).wait_recv()
        acc[...] += pair_in[place].astype(F32)

    def chip_add(i, carry):
        rc(part_out.at[place], chip_in.at[i], part_s.at[place], chip_r.at[i], at_place(2 * i + core)).wait_recv()
        acc[...] += chip_in[i].astype(F32)
        return carry

    lax.fori_loop(chip + 1, QUAD, chip_add, 0)
    key_grad = unrotate(acc[0] * score_scale).astype(BF16)
    value_grad = acc[1].astype(BF16)
    dk_ref[...] = key_grad
    dv_ref[...] = value_grad
    back_out[8:16, :] = dot_nt(ukv_ref[0:8, :], key_grad).astype(BF16)
    back_out[16:24, :] = dot_nt(ukv_ref[8:16, :], value_grad).astype(BF16)
    back_in[h] = back_out[...]
    head_loop(lambda i: rc(back_out, back_in.at[h], back_s.at[i], back_r.at[h], at_head(i)).start())

    def summed(ref, count):
        total = ref[0].astype(F32)
        for i in range(1, count):
            total = total + ref[i].astype(F32)
        return total

    def unit_loop(fn):
        for i in range(1, QUAD):
            fn((unit + i) % QUAD)

    def z_loop(fn):
        lax.fori_loop(1, z_count, lambda i, c: (fn((z + i) % z_count), c)[1], 0)

    class Reduce:
        def __init__(self, ro, ri, zo, zi, go, gi, rss, rsr, zs, zr, gs, gr):
            self.refs = (ro, ri, zo, zi, go, gi)
            self.rs = lambda i: rc(ro.at[i], ri.at[unit], rss.at[i], rsr.at[unit], at_unit(i))
            self.rw = lambda i: rc(ro.at[i], ri.at[i], rss.at[i], rsr.at[i], at_unit(i))
            self.zs = lambda i: rc(zo, zi.at[z], zs.at[i], zr.at[z], at_z(i))
            self.zw = lambda i: rc(zo, zi.at[i], zs.at[i], zr.at[i], at_z(i))
            self.gs = lambda i: rc(go, gi.at[unit], gs.at[i], gr.at[unit], at_unit(i))
            self.gw = lambda i: rc(go, gi.at[i], gs.at[i], gr.at[i], at_unit(i))

        def scatter(self):
            ro, ri = self.refs[:2]
            unit_loop(lambda i: self.rs(i).start())
            ri[unit] = ro[unit]

        def across(self):
            ro, ri, zo, zi = self.refs[:4]
            unit_loop(lambda i: self.rw(i).wait_recv())
            zo[...] = summed(ri, QUAD).astype(BF16)
            z_loop(lambda i: self.zs(i).start())
            zi[z] = zo[...]

        def gather(self):
            zi, go, gi = self.refs[3:]
            z_loop(lambda i: self.zw(i).wait_recv())
            go[...] = summed(zi, z_count).astype(BF16)
            unit_loop(lambda i: self.gs(i).start())
            gi[unit] = go[...]

        def finish(self):
            unit_loop(lambda i: self.gw(i).wait_recv())

        def drain(self):
            unit_loop(lambda i: self.rw(i).wait_send())
            z_loop(lambda i: self.zw(i).wait_send())
            unit_loop(lambda i: self.gw(i).wait_send())

    first = Reduce(rs1_out, rs1_in, z1_out, z1_in, g1_out, g1_in, rs1_s, rs1_r, z1_s, z1_r, g1_s, g1_r)
    second = Reduce(rs2_out, rs2_in, z2_out, z2_in, g2_out, g2_in, rs2_s, rs2_r, z2_s, z2_r, g2_s, g2_r)

    head_loop(lambda i: rc(down_out, down_in.at[i], down_s.at[i], down_r.at[i], at_head(i)).wait_recv())
    down_act = summed(down_in, head_count).astype(BF16)
    up_query = (2.0 * dot(down_act[0:8, :], dq_ref[...])).astype(BF16)
    up_key = (2.0 * dot(down_act[8:16, :], key_grad)).astype(BF16)
    up_value = (2.0 * dot(down_act[16:24, :], value_grad)).astype(BF16)
    chunk = width // QUAD
    for i in range(QUAD):
        rs1_out[i, 0:8, :] = up_query[:, i * chunk : (i + 1) * chunk]
        rs1_out[i, 8:16, 0:HEAD_SIZE] = up_key
        rs1_out[i, 8:16, HEAD_SIZE:] = up_value
    first.scatter()
    first.across()

    head_loop(lambda i: rc(back_out, back_in.at[i], back_s.at[i], back_r.at[i], at_head(i)).wait_recv())
    back_act = summed(back_in, head_count).astype(BF16)
    down_grad = (2.0 * dot(back_act, x_ref[...])).astype(BF16)
    for i in range(QUAD):
        rs2_out[i] = down_grad[:, i * chunk : (i + 1) * chunk]
    second.scatter()
    second.across()
    first.gather()
    second.gather()
    first.finish()
    for i in range(QUAD):
        guq_ref[:, i * chunk : (i + 1) * chunk] = g1_in[i, 0:8, :].astype(F32)
    gukv_ref[0:8, :] = g1_out[8:16, 0:HEAD_SIZE].astype(F32)
    gukv_ref[8:16, :] = g1_out[8:16, HEAD_SIZE:].astype(F32)
    second.finish()
    for i in range(QUAD):
        gd_ref[:, i * chunk : (i + 1) * chunk] = g2_in[i].astype(F32)

    @pl.when(core == 0)
    def _():
        kv_copy(place + 1).wait_send()

    lax.fori_loop(chip + 1, QUAD, lambda i, c: (kv_copy(2 * i + core).wait_send(), c)[1], 0)

    def drain_block(i, carry):
        j = 2 * i + core
        rc(kv_all.at[j], kv_all.at[j], fw_s.at[j], kv_r.at[j], partner).wait_send()
        return carry

    lax.fori_loop(0, chip, drain_block, 0)
    lax.fori_loop(0, place, lambda j, c: (part_copy_pair(j).wait_send(), c)[1], 0)
    head_loop(lambda i: rc(down_out, down_in.at[i], down_s.at[i], down_r.at[i], at_head(i)).wait_send())
    head_loop(lambda i: rc(back_out, back_in.at[i], back_s.at[i], back_r.at[i], at_head(i)).wait_send())
    first.drain()
    second.drain()


def body(x, q, k, v, do, wd, uq, ukv):
    rows, width = q.shape
    seq_count = lax.axis_size("seq")
    head_count = lax.axis_size("head")
    heads = width // HEAD_SIZE
    features = x.shape[1]
    chunk = width // QUAD
    z_count = seq_count // QUAD
    vmem = pl.BlockSpec(memory_space=pltpu.VMEM)
    dma = pltpu.SemaphoreType.DMA
    reduce_bufs = []
    for depth in (16, 24):
        reduce_bufs += [
            pltpu.VMEM((QUAD, depth, chunk), BF16),
            pltpu.VMEM((QUAD, depth, chunk), BF16),
            pltpu.VMEM((depth, chunk), BF16),
            pltpu.VMEM((z_count, depth, chunk), BF16),
            pltpu.VMEM((depth, chunk), BF16),
            pltpu.VMEM((QUAD, depth, chunk), BF16),
        ]
    reduce_sems = [dma((n,)) for n in (QUAD, QUAD, z_count, z_count, QUAD, QUAD)] * 2
    outs = pl.pallas_call(
        functools.partial(kernel, seq_count, head_count),
        out_shape=(
            jax.ShapeDtypeStruct((rows, width), BF16),
            jax.ShapeDtypeStruct((rows, HEAD_SIZE), BF16),
            jax.ShapeDtypeStruct((rows, HEAD_SIZE), BF16),
            jax.ShapeDtypeStruct((24, features), F32),
            jax.ShapeDtypeStruct((8, width), F32),
            jax.ShapeDtypeStruct((16, HEAD_SIZE), F32),
        ),
        in_specs=[vmem] * 8,
        out_specs=(vmem,) * 6,
        scratch_shapes=[
            pltpu.VMEM((GROUP, 2, rows, HEAD_SIZE), BF16),
            pltpu.VMEM((GROUP, HEAD_SIZE, rows), BF16),
            pltpu.VMEM((heads * rows, HEAD_SIZE), BF16),
            pltpu.VMEM((heads * rows, HEAD_SIZE), BF16),
            pltpu.VMEM((GROUP, rows, heads * rows), F32),
            pltpu.VMEM((GROUP, rows, heads * rows), F32),
            pltpu.VMEM((GROUP, heads, 1, rows), F32),
            pltpu.VMEM((heads, 1, rows), F32),
            pltpu.VMEM((heads, 1, rows), F32),
            pltpu.VMEM((heads, 1, rows), F32),
            pltpu.VMEM((rows, heads * rows), BF16),
            pltpu.VMEM((rows, heads * rows), BF16),
            pltpu.VMEM((HEAD_SIZE, heads * rows), F32),
            pltpu.VMEM((2, rows, HEAD_SIZE), F32),
            pltpu.VMEM((GROUP, 2, rows, HEAD_SIZE), BF16),
            pltpu.VMEM((GROUP, 2, rows, HEAD_SIZE), BF16),
            pltpu.VMEM((QUAD, 2, rows, HEAD_SIZE), BF16),
            pltpu.VMEM((24, rows), BF16),
            pltpu.VMEM((head_count, 24, rows), BF16),
            pltpu.VMEM((24, rows), BF16),
            pltpu.VMEM((head_count, 24, rows), BF16),
        ]
        + reduce_bufs
        + [dma((GROUP,)), dma((GROUP,)), dma((GROUP,)), dma((GROUP,)), dma((GROUP,)), dma((QUAD,))]
        + [dma((head_count,))] * 4
        + reduce_sems,
        compiler_params=pltpu.CompilerParams(
            collective_id=0, has_side_effects=True, vmem_limit_bytes=60 * 1024 * 1024
        ),
    )(
        q,
        k,
        v,
        do,
        x,
        wd.reshape(24, features),
        uq,
        ukv.reshape(16, HEAD_SIZE),
    )
    dq, dk, dv, gd, guq, gukv = outs
    return (dq, dk, dv, gd.reshape(3, 8, features), guq, gukv.reshape(2, 8, HEAD_SIZE))


def solution(mesh):
    tokens = P("seq", "head")
    return jax.shard_map(
        body,
        mesh=mesh,
        in_specs=(tokens,) * 5 + (P(None, None, "head"), P(None, "head"), P(None, None, "head")),
        out_specs=(tokens,) * 3 + (P(None, None, "head"), P(None, "head"), P(None, None, "head")),
        check_vma=False,
    )
```

```python
import functools

import jax
import jax.numpy as jnp
from jax import lax
from jax.experimental import pallas as pl
from jax.experimental.pallas import tpu as pltpu
from jax.sharding import PartitionSpec as P

HEAD_SIZE = 128
POSITION_SCALE = 0.04096
LOG2E = 1.4426950408889634
MESH = pl.DeviceIdType.MESH
F32 = jnp.float32
BF16 = jnp.bfloat16
GROUP = 8
QUAD = 4
WIDE = 2
NT = (((1,), (1,)), ((), ()))


def dot(a, b):
    return jnp.dot(a, b, preferred_element_type=F32)


def dot_nt(a, b):
    return lax.dot_general(a, b, NT, preferred_element_type=F32)


def kernel(
    seq_count,
    head_count,
    q_hbm,
    k_hbm,
    v_hbm,
    do_hbm,
    x_hbm,
    wd_hbm,
    uq_hbm,
    ukv_hbm,
    dq_ref,
    dk_ref,
    dv_ref,
    gd_ref,
    guq_ref,
    gukv_ref,
    q_ref,
    k_ref,
    do_ref,
    x_ref,
    wd_ref,
    uq_ref,
    ukv_ref,
    kv_all,
    kt_all,
    q_rot,
    do_hm,
    dqt_b,
    e_buf,
    dp_buf,
    m_blk,
    m_run,
    l_run,
    d_run,
    p_t,
    ds_t,
    dq_t,
    acc,
    part_out,
    pair_in,
    chip_in,
    down_out,
    down_in,
    back_out,
    back_in,
    rs1_out,
    rs1_in,
    z1_out,
    z1_in,
    g1_out,
    g1_in,
    rs2_out,
    rs2_in,
    z2_out,
    z2_in,
    g2_out,
    g2_in,
    z_hop,
    x_hop,
    in_s,
    kv_s,
    kv_r,
    fw_s,
    part_s,
    pair_r,
    chip_r,
    down_s,
    down_r,
    back_s,
    back_r,
    rs1_s,
    rs1_r,
    z1_s,
    z1_r,
    g1_s,
    g1_r,
    rs2_s,
    rs2_r,
    z2_s,
    z2_r,
    g2_s,
    g2_r,
):
    rows = k_ref.shape[0]
    heads = q_ref.shape[1] // HEAD_SIZE
    width = heads * HEAD_SIZE
    score_scale = HEAD_SIZE ** -0.5
    s = lax.axis_index("seq")
    h = lax.axis_index("head")
    shift = jnp.where(h >= head_count // 2, GROUP // 2, 0)
    place = (s + seq_count - shift) % GROUP
    chip = place // 2
    core = place % 2
    unit = s % QUAD
    z = s // QUAD
    z_count = seq_count // QUAD

    def at_place(q):
        return ((s + seq_count - place + q) % seq_count, h)

    partner = at_place(place + 1 - 2 * core)

    def at_head(i):
        return (s, i)

    def at_unit(i):
        return (z * QUAD + i, h)

    def at_z(i):
        return (i * QUAD + unit, h)

    def rc(src, dst, ss, rs, dev):
        return pltpu.make_async_remote_copy(
            src_ref=src, dst_ref=dst, send_sem=ss, recv_sem=rs, device_id=dev, device_id_type=MESH
        )

    barrier = pltpu.get_barrier_semaphore()

    def signal(sem, dev):
        pl.semaphore_signal(sem, inc=1, device_id=dev, device_id_type=MESH)

    x_count = head_count // 2
    x_base = h - h % x_count
    z_near = (at_z((z + 1) % z_count), at_z((z + z_count - 1) % z_count))
    x_near = (
        at_head(x_base + (h + 1) % x_count),
        at_head(x_base + (h + x_count - 1) % x_count),
    )

    lax.fori_loop(1, GROUP, lambda i, c: (signal(barrier, at_place((place + i) % GROUP)), c)[1], 0)
    for dev in z_near + x_near + (at_head((h + x_count) % head_count),):
        signal(barrier, dev)

    def z_tell(n):
        for dev in z_near:
            signal(z_hop.at[n], dev)

    def x_tell(n):
        for dev in x_near:
            signal(x_hop.at[n], dev)

    loads = [
        pltpu.make_async_copy(src, dst, in_s.at[i])
        for i, (src, dst) in enumerate(
            (
                (k_hbm, k_ref),
                (v_hbm, kv_all.at[place, 1]),
                (q_hbm, q_ref),
                (do_hbm, do_ref),
                (x_hbm, x_ref),
                (wd_hbm, wd_ref),
                (uq_hbm, uq_ref),
                (ukv_hbm, ukv_ref),
            )
        )
    ]
    for load in loads:
        load.start()

    half = HEAD_SIZE // 2
    feature = lax.broadcasted_iota(jnp.int32, (half, 1), 0).astype(F32)
    frequency = POSITION_SCALE * jnp.exp(feature * (-2.0 / HEAD_SIZE * 9.210340371976184))
    position = (s * rows + lax.broadcasted_iota(jnp.int32, (1, rows), 1)).astype(F32)
    angle = frequency * position
    cosine = jnp.cos(angle)
    sine = jnp.sin(angle)

    def turned(x, sn):
        lo = x[:half, :]
        hi = x[half:, :]
        return jnp.concatenate([lo * cosine - hi * sn, hi * cosine + lo * sn], axis=0).astype(BF16)

    loads[0].wait()
    loads[1].wait()
    own_t = turned(k_ref[...].T.astype(F32), sine)
    kt_all[place] = own_t
    kv_all[place, 0] = own_t.T
    pl.semaphore_wait(barrier, 12)

    def kv_copy(q):
        return rc(kv_all.at[place], kv_all.at[place], kv_s.at[q], kv_r.at[place], at_place(q))

    @pl.when(core == 0)
    def _():
        kv_copy(place + 1).start()

    def kv_start(i, carry):
        kv_copy(2 * i + core).start()
        return carry

    lax.fori_loop(chip + 1, QUAD, kv_start, 0)
    z_tell(0)
    x_tell(0)

    loads[2].wait()
    loads[3].wait()
    for i in range(heads):
        cols = slice(i * HEAD_SIZE, (i + 1) * HEAD_SIZE)
        span = slice(i * rows, (i + 1) * rows)
        q_rot[span, :] = turned(q_ref[:, cols].T.astype(F32), sine).T
        do_hm[span, :] = do_ref[:, cols]

    def head_loop(fn):
        lax.fori_loop(1, head_count, lambda i, c: (fn((h + i) % head_count), c)[1], 0)

    def forward_block(j, masked):
        keys = kv_all[j, 0]
        values = kv_all[j, 1]
        if not masked:
            kt_all[j] = keys.T
        for i in range(heads):
            span = slice(i * rows, (i + 1) * rows)
            if i % WIDE == 0:
                part = slice(i * rows, (i + WIDE) * rows)
                st_wide = dot_nt(keys, q_rot[part, :])
                dp_wide = dot_nt(values, do_hm[part, :])
            here = slice((i % WIDE) * rows, (i % WIDE + 1) * rows)
            st = st_wide[:, here]
            dp = dp_wide[:, here]
            if masked:
                key_pos = lax.broadcasted_iota(jnp.int32, (rows, rows), 0)
                query_pos = lax.broadcasted_iota(jnp.int32, (rows, rows), 1)
                st = jnp.where(key_pos <= query_pos, st, -1e30)
                top = jnp.max(st, axis=0, keepdims=True)
                e = jnp.exp2((st - top) * (score_scale * LOG2E))
                l_run[i] = jnp.sum(e, axis=0, keepdims=True)
                d_run[i] = jnp.sum(e * dp, axis=0, keepdims=True)
            else:
                old = m_run[i]
                top = jnp.maximum(old, jnp.max(st, axis=0, keepdims=True))
                e = jnp.exp2((st - top) * (score_scale * LOG2E))
                fix = jnp.exp2((old - top) * (score_scale * LOG2E))
                l_run[i] = l_run[i] * fix + jnp.sum(e, axis=0, keepdims=True)
                d_run[i] = d_run[i] * fix + jnp.sum(e * dp, axis=0, keepdims=True)
            m_run[i] = top
            m_blk[j, i] = top
            e_buf[j, :, span] = e
            dp_buf[j, :, span] = dp

    pl.semaphore_wait(x_hop.at[0], 2)
    x_tell(1)
    pl.semaphore_wait(z_hop.at[0], 2)
    z_tell(1)
    forward_block(place, True)
    pl.semaphore_wait(x_hop.at[1], 2)
    pl.semaphore_wait(z_hop.at[1], 2)
    z_tell(2)

    for load in loads[4:]:
        load.wait()
    down_out[...] = dot_nt(wd_ref[...], x_ref[...]).astype(BF16)
    down_in[h] = down_out[...]
    head_loop(lambda i: rc(down_out, down_in.at[h], down_s.at[i], down_r.at[h], at_head(i)).start())

    def kv_arrived(j):
        rc(kv_all.at[j], kv_all.at[j], kv_s.at[j], kv_r.at[j], partner).wait_recv()

    def relay(j):
        kv_arrived(j)
        rc(kv_all.at[j], kv_all.at[j], fw_s.at[j], kv_r.at[j], partner).start()

    @pl.when(core == 1)
    def _():
        kv_arrived(place - 1)
        forward_block(place - 1, False)

    @pl.when(chip > 0)
    def _():
        relay(place - 2)

    def forward_step(n, carry):
        i = n // 2
        par = n % 2
        base = 2 * (chip - 1 - i)

        @pl.when(par == 1)
        def _():
            @pl.when(i < chip - 1)
            def _():
                relay(base - 2 + core)

            kv_arrived(base + 1 - core)

        forward_block(base + core + par * (1 - 2 * core), False)
        return carry

    lax.fori_loop(0, 2 * chip, forward_step, 0)

    pl.semaphore_wait(z_hop.at[2], 2)
    for i in range(heads):
        inv = 1.0 / l_run[i]
        l_run[i] = inv
        d_run[i] = d_run[i] * inv

    dq_t[...] = jnp.zeros_like(dq_t)

    def backward_block(j):
        for i in range(heads):
            span = slice(i * rows, (i + 1) * rows)
            scale = jnp.exp2((m_blk[j, i] - m_run[i]) * (score_scale * LOG2E)) * l_run[i]
            prob = e_buf[j, :, span] * scale
            p_t[:, span] = prob.astype(BF16)
            ds_t[:, span] = (prob * (dp_buf[j, :, span] - d_run[i])).astype(BF16)
            if i % 4 == 3:
                part = slice((i - 3) * rows, (i + 1) * rows)
                key_new = dot(ds_t[:, part], q_rot[part, :])
                value_new = dot(p_t[:, part], do_hm[part, :])
                key_part = key_new if i == 3 else key_part + key_new
                value_part = value_new if i == 3 else value_part + value_new
        dq_t[...] += dot(kt_all[j], ds_t[...])
        return key_part, value_part

    def part_copy_pair(j):
        return rc(part_out.at[j], pair_in.at[j], part_s.at[j], pair_r.at[j], partner)

    def part_copy_chip(j):
        return rc(part_out.at[j], chip_in.at[chip], part_s.at[j], chip_r.at[chip], at_place(j))

    def backward_step(w, carry):
        par = w % 2
        j = 2 * (w // 2) + (1 - core) + par * (2 * core - 1)
        key_part, value_part = backward_block(j)

        @pl.when(par == 0)
        def _():
            part_out[j, 0] = key_part.astype(BF16)
            part_out[j, 1] = value_part.astype(BF16)
            part_copy_pair(j).start()

        @pl.when(par == 1)
        def _():
            part_copy_pair(j).wait_recv()
            part_out[j, 0] = (key_part + pair_in[j, 0].astype(F32)).astype(BF16)
            part_out[j, 1] = (value_part + pair_in[j, 1].astype(F32)).astype(BF16)
            part_copy_chip(j).start()

        return carry

    lax.fori_loop(0, place, backward_step, 0)
    key_part, value_part = backward_block(place)
    acc[0] = key_part
    acc[1] = value_part

    for i in range(heads):
        span = slice(i * rows, (i + 1) * rows)
        cols = slice(i * HEAD_SIZE, (i + 1) * HEAD_SIZE)
        grad = turned(dq_t[:, span] * score_scale, -sine)
        dqt_b[cols, :] = grad
        dq_ref[:, cols] = grad.T
    back_out[0:8, :] = dot(uq_ref[...], dqt_b[...]).astype(BF16)

    @pl.when(core == 0)
    def _():
        rc(part_out.at[place], pair_in.at[place], part_s.at[place], pair_r.at[place], partner).wait_recv()
        acc[...] += pair_in[place].astype(F32)

    def chip_add(i, carry):
        rc(part_out.at[place], chip_in.at[i], part_s.at[place], chip_r.at[i], at_place(2 * i + core)).wait_recv()
        acc[...] += chip_in[i].astype(F32)
        return carry

    lax.fori_loop(chip + 1, QUAD, chip_add, 0)
    key_grad = turned(acc[0].T * score_scale, -sine)
    dv_ref[...] = acc[1].astype(BF16)
    back_out[8:16, :] = dot(ukv_ref[0:8, :], key_grad).astype(BF16)
    back_out[16:24, :] = dot_nt(ukv_ref[8:16, :], dv_ref[...]).astype(BF16)
    back_in[h] = back_out[...]
    head_loop(lambda i: rc(back_out, back_in.at[h], back_s.at[i], back_r.at[h], at_head(i)).start())

    def summed(ref, count):
        total = ref[0].astype(F32)
        for i in range(1, count):
            total = total + ref[i].astype(F32)
        return total

    def unit_loop(fn):
        for i in range(1, QUAD):
            fn((unit + i) % QUAD)

    def z_loop(fn):
        lax.fori_loop(1, z_count, lambda i, c: (fn((z + i) % z_count), c)[1], 0)

    class Reduce:
        def __init__(self, ro, ri, zo, zi, go, gi, rss, rsr, zs, zr, gs, gr):
            self.refs = (ro, ri, zo, zi, go, gi)
            self.rs = lambda i: rc(ro.at[i], ri.at[unit], rss.at[i], rsr.at[unit], at_unit(i))
            self.rw = lambda i: rc(ro.at[i], ri.at[i], rss.at[i], rsr.at[i], at_unit(i))
            self.zs = lambda i: rc(zo, zi.at[z], zs.at[i], zr.at[z], at_z(i))
            self.zw = lambda i: rc(zo, zi.at[i], zs.at[i], zr.at[i], at_z(i))
            self.gs = lambda i: rc(go, gi.at[unit], gs.at[i], gr.at[unit], at_unit(i))
            self.gw = lambda i: rc(go, gi.at[i], gs.at[i], gr.at[i], at_unit(i))

        def scatter(self):
            ro, ri = self.refs[:2]
            unit_loop(lambda i: self.rs(i).start())
            ri[unit] = ro[unit]

        def across(self):
            ro, ri, zo, zi = self.refs[:4]
            unit_loop(lambda i: self.rw(i).wait_recv())
            zo[...] = summed(ri, QUAD).astype(BF16)
            z_loop(lambda i: self.zs(i).start())
            zi[z] = zo[...]

        def gather(self):
            zi, go, gi = self.refs[3:]
            z_loop(lambda i: self.zw(i).wait_recv())
            go[...] = summed(zi, z_count).astype(BF16)
            unit_loop(lambda i: self.gs(i).start())
            gi[unit] = go[...]

        def finish(self):
            unit_loop(lambda i: self.gw(i).wait_recv())

        def drain(self):
            unit_loop(lambda i: self.rw(i).wait_send())
            z_loop(lambda i: self.zw(i).wait_send())
            unit_loop(lambda i: self.gw(i).wait_send())

    first = Reduce(rs1_out, rs1_in, z1_out, z1_in, g1_out, g1_in, rs1_s, rs1_r, z1_s, z1_r, g1_s, g1_r)
    second = Reduce(rs2_out, rs2_in, z2_out, z2_in, g2_out, g2_in, rs2_s, rs2_r, z2_s, z2_r, g2_s, g2_r)

    dk_ref[...] = key_grad.T

    head_loop(lambda i: rc(down_out, down_in.at[i], down_s.at[i], down_r.at[i], at_head(i)).wait_recv())
    down_act = summed(down_in, head_count).astype(BF16)
    up_query = (2.0 * dot(down_act[0:8, :], dq_ref[...])).astype(BF16)
    up_key = (2.0 * dot(down_act[8:16, :], dk_ref[...])).astype(BF16)
    up_value = (2.0 * dot(down_act[16:24, :], dv_ref[...])).astype(BF16)
    chunk = width // QUAD
    for i in range(QUAD):
        rs1_out[i, 0:8, :] = up_query[:, i * chunk : (i + 1) * chunk]
        rs1_out[i, 8:16, 0:HEAD_SIZE] = up_key
        rs1_out[i, 8:16, HEAD_SIZE:] = up_value
    first.scatter()
    first.across()

    head_loop(lambda i: rc(back_out, back_in.at[i], back_s.at[i], back_r.at[i], at_head(i)).wait_recv())
    back_act = summed(back_in, head_count).astype(BF16)
    down_grad = (2.0 * dot(back_act, x_ref[...])).astype(BF16)
    for i in range(QUAD):
        rs2_out[i] = down_grad[:, i * chunk : (i + 1) * chunk]
    second.scatter()
    second.across()
    first.gather()
    second.gather()
    first.finish()
    for i in range(QUAD):
        guq_ref[:, i * chunk : (i + 1) * chunk] = g1_in[i, 0:8, :].astype(F32)
    gukv_ref[0:8, :] = g1_out[8:16, 0:HEAD_SIZE].astype(F32)
    gukv_ref[8:16, :] = g1_out[8:16, HEAD_SIZE:].astype(F32)
    second.finish()
    for i in range(QUAD):
        gd_ref[:, i * chunk : (i + 1) * chunk] = g2_in[i].astype(F32)

    @pl.when(core == 0)
    def _():
        kv_copy(place + 1).wait_send()

    lax.fori_loop(chip + 1, QUAD, lambda i, c: (kv_copy(2 * i + core).wait_send(), c)[1], 0)

    def drain_block(i, carry):
        j = 2 * i + core
        rc(kv_all.at[j], kv_all.at[j], fw_s.at[j], kv_r.at[j], partner).wait_send()
        return carry

    lax.fori_loop(0, chip, drain_block, 0)
    lax.fori_loop(0, place, lambda j, c: (part_copy_pair(j).wait_send(), c)[1], 0)
    head_loop(lambda i: rc(down_out, down_in.at[i], down_s.at[i], down_r.at[i], at_head(i)).wait_send())
    head_loop(lambda i: rc(back_out, back_in.at[i], back_s.at[i], back_r.at[i], at_head(i)).wait_send())
    first.drain()
    second.drain()


def hand_over(*refs):
    copies = [pltpu.make_async_copy(refs[i], refs[6 + i], refs[12].at[i]) for i in range(6)]
    for copy in copies:
        copy.start()
    for copy in copies:
        copy.wait()


def body(x, q, k, v, do, wd, uq, ukv):
    rows, width = q.shape
    seq_count = lax.axis_size("seq")
    head_count = lax.axis_size("head")
    heads = width // HEAD_SIZE
    features = x.shape[1]
    chunk = width // QUAD
    z_count = seq_count // QUAD
    vmem = pl.BlockSpec(memory_space=pltpu.VMEM)
    hbm = pl.BlockSpec(memory_space=pl.ANY)
    dma = pltpu.SemaphoreType.DMA
    reduce_bufs = []
    for depth in (16, 24):
        reduce_bufs += [
            pltpu.VMEM((QUAD, depth, chunk), BF16),
            pltpu.VMEM((QUAD, depth, chunk), BF16),
            pltpu.VMEM((depth, chunk), BF16),
            pltpu.VMEM((z_count, depth, chunk), BF16),
            pltpu.VMEM((depth, chunk), BF16),
            pltpu.VMEM((QUAD, depth, chunk), BF16),
        ]
    reduce_sems = [dma((n,)) for n in (QUAD, QUAD, z_count, z_count, QUAD, QUAD)] * 2
    outs = pl.pallas_call(
        functools.partial(kernel, seq_count, head_count),
        out_shape=(
            pltpu.VMEM((rows, width), BF16),
            pltpu.VMEM((rows, HEAD_SIZE), BF16),
            pltpu.VMEM((rows, HEAD_SIZE), BF16),
            pltpu.VMEM((24, features), F32),
            pltpu.VMEM((8, width), F32),
            pltpu.VMEM((16, HEAD_SIZE), F32),
        ),
        in_specs=[hbm] * 8,
        out_specs=(vmem,) * 6,
        scratch_shapes=[
            pltpu.VMEM((rows, width), BF16),
            pltpu.VMEM((rows, HEAD_SIZE), BF16),
            pltpu.VMEM((rows, width), BF16),
            pltpu.VMEM((rows, features), BF16),
            pltpu.VMEM((24, features), BF16),
            pltpu.VMEM((8, width), BF16),
            pltpu.VMEM((16, HEAD_SIZE), BF16),
            pltpu.VMEM((GROUP, 2, rows, HEAD_SIZE), BF16),
            pltpu.VMEM((GROUP, HEAD_SIZE, rows), BF16),
            pltpu.VMEM((heads * rows, HEAD_SIZE), BF16),
            pltpu.VMEM((heads * rows, HEAD_SIZE), BF16),
            pltpu.VMEM((width, rows), BF16),
            pltpu.VMEM((GROUP, rows, heads * rows), F32),
            pltpu.VMEM((GROUP, rows, heads * rows), F32),
            pltpu.VMEM((GROUP, heads, 1, rows), F32),
            pltpu.VMEM((heads, 1, rows), F32),
            pltpu.VMEM((heads, 1, rows), F32),
            pltpu.VMEM((heads, 1, rows), F32),
            pltpu.VMEM((rows, heads * rows), BF16),
            pltpu.VMEM((rows, heads * rows), BF16),
            pltpu.VMEM((HEAD_SIZE, heads * rows), F32),
            pltpu.VMEM((2, rows, HEAD_SIZE), F32),
            pltpu.VMEM((GROUP, 2, rows, HEAD_SIZE), BF16),
            pltpu.VMEM((GROUP, 2, rows, HEAD_SIZE), BF16),
            pltpu.VMEM((QUAD, 2, rows, HEAD_SIZE), BF16),
            pltpu.VMEM((24, rows), BF16),
            pltpu.VMEM((head_count, 24, rows), BF16),
            pltpu.VMEM((24, rows), BF16),
            pltpu.VMEM((head_count, 24, rows), BF16),
        ]
        + reduce_bufs
        + [pltpu.SemaphoreType.REGULAR((3,)), pltpu.SemaphoreType.REGULAR((2,))]
        + [dma((8,))]
        + [dma((GROUP,))] * 5
        + [dma((QUAD,))]
        + [dma((head_count,))] * 4
        + reduce_sems,
        compiler_params=pltpu.CompilerParams(
            collective_id=0, has_side_effects=True, vmem_limit_bytes=54 * 1024 * 1024
        ),
    )(
        q,
        k,
        v,
        do,
        x,
        wd.reshape(24, features),
        uq,
        ukv.reshape(16, HEAD_SIZE),
    )
    dq, dk, dv, gd, guq, gukv = pl.pallas_call(
        hand_over,
        out_shape=tuple(jax.ShapeDtypeStruct(o.shape, o.dtype) for o in outs),
        in_specs=[vmem] * 6,
        out_specs=(hbm,) * 6,
        scratch_shapes=[dma((6,))],
    )(*[pltpu.with_memory_space_constraint(o, pltpu.VMEM) for o in outs])
    return (dq, dk, dv, gd.reshape(3, 8, features), guq, gukv.reshape(2, 8, HEAD_SIZE))


def solution(mesh):
    tokens = P("seq", "head")
    return jax.shard_map(
        body,
        mesh=mesh,
        in_specs=(tokens,) * 5 + (P(None, None, "head"), P(None, "head"), P(None, None, "head")),
        out_specs=(tokens,) * 3 + (P(None, None, "head"), P(None, "head"), P(None, None, "head")),
        check_vma=False,
    )
```

```python
import functools

import jax
import jax.numpy as jnp
from jax import lax
from jax.experimental import pallas as pl
from jax.experimental.pallas import tpu as pltpu
from jax.sharding import PartitionSpec as P

HEAD_SIZE = 128
POSITION_SCALE = 0.04096
LOG2E = 1.4426950408889634
MESH = pl.DeviceIdType.MESH
F32 = jnp.float32
BF16 = jnp.bfloat16
GROUP = 8
QUAD = 4
WIDE = 2
NT = (((1,), (1,)), ((), ()))


def dot(a, b):
    return jnp.dot(a, b, preferred_element_type=F32)


def dot_nt(a, b):
    return lax.dot_general(a, b, NT, preferred_element_type=F32)


def kernel(
    seq_count,
    head_count,
    q_hbm,
    k_hbm,
    v_hbm,
    do_hbm,
    x_hbm,
    wd_hbm,
    uq_hbm,
    ukv_hbm,
    dq_ref,
    dk_ref,
    dv_ref,
    gd_ref,
    guq_ref,
    gukv_ref,
    q_ref,
    k_ref,
    do_ref,
    x_ref,
    wd_ref,
    uq_ref,
    ukv_ref,
    kv_all,
    kt_all,
    q_rot,
    do_hm,
    dqt_b,
    e_buf,
    dp_buf,
    m_blk,
    m_run,
    l_run,
    d_run,
    p_t,
    ds_t,
    dq_t,
    acc,
    part_out,
    pair_in,
    chip_in,
    table,
    mini_out,
    mini_in,
    back_kv,
    down_out,
    down_in,
    back_out,
    back_in,
    rs1_out,
    rs1_in,
    z1_out,
    z1_in,
    g1_out,
    g1_in,
    rs2_out,
    rs2_in,
    z2_out,
    z2_in,
    g2_out,
    g2_in,
    z_hop,
    x_hop,
    in_s,
    kv_s,
    kv_r,
    fw_s,
    part_s,
    pair_r,
    chip_r,
    mini_s,
    mini_r,
    down_s,
    down_r,
    back_s,
    back_r,
    rs1_s,
    rs1_r,
    z1_s,
    z1_r,
    g1_s,
    g1_r,
    rs2_s,
    rs2_r,
    z2_s,
    z2_r,
    g2_s,
    g2_r,
):
    rows = k_ref.shape[0]
    heads = q_ref.shape[1] // HEAD_SIZE
    width = heads * HEAD_SIZE
    score_scale = HEAD_SIZE ** -0.5
    s = lax.axis_index("seq")
    h = lax.axis_index("head")
    shift = jnp.where(h >= head_count // 2, GROUP // 2, 0)
    place = (s + seq_count - shift) % GROUP
    chip = place // 2
    core = place % 2
    unit = s % QUAD
    z = s // QUAD
    z_count = seq_count // QUAD

    def at_place(q):
        return ((s + seq_count - place + q) % seq_count, h)

    partner = at_place(place + 1 - 2 * core)

    def at_head(i):
        return (s, i)

    def at_unit(i):
        return (z * QUAD + i, h)

    def at_z(i):
        return (i * QUAD + unit, h)

    def rc(src, dst, ss, rs, dev):
        return pltpu.make_async_remote_copy(
            src_ref=src, dst_ref=dst, send_sem=ss, recv_sem=rs, device_id=dev, device_id_type=MESH
        )

    barrier = pltpu.get_barrier_semaphore()

    def signal(sem, dev):
        pl.semaphore_signal(sem, inc=1, device_id=dev, device_id_type=MESH)

    x_count = head_count // 2
    x_base = h - h % x_count
    z_near = (at_z((z + 1) % z_count), at_z((z + z_count - 1) % z_count))
    x_near = (
        at_head(x_base + (h + 1) % x_count),
        at_head(x_base + (h + x_count - 1) % x_count),
    )

    lax.fori_loop(1, GROUP, lambda i, c: (signal(barrier, at_place((place + i) % GROUP)), c)[1], 0)
    for dev in z_near + x_near + (at_head((h + x_count) % head_count),):
        signal(barrier, dev)

    def z_tell(n):
        for dev in z_near:
            signal(z_hop.at[n], dev)

    def x_tell(n):
        for dev in x_near:
            signal(x_hop.at[n], dev)

    loads = [
        pltpu.make_async_copy(src, dst, in_s.at[i])
        for i, (src, dst) in enumerate(
            (
                (k_hbm, k_ref),
                (v_hbm, kv_all.at[place, 1]),
                (q_hbm, q_ref),
                (do_hbm, do_ref),
                (x_hbm, x_ref),
                (wd_hbm, wd_ref),
                (uq_hbm, uq_ref),
                (ukv_hbm, ukv_ref),
            )
        )
    ]
    for load in loads:
        load.start()

    half = HEAD_SIZE // 2
    feature = lax.broadcasted_iota(jnp.int32, (half, 1), 0).astype(F32)
    frequency = POSITION_SCALE * jnp.exp(feature * (-2.0 / HEAD_SIZE * 9.210340371976184))
    position = (s * rows + lax.broadcasted_iota(jnp.int32, (1, rows), 1)).astype(F32)
    angle = frequency * position
    cosine = jnp.cos(angle)
    sine = jnp.sin(angle)

    def turned_by(x, cs, sn):
        lo = x[:half, :]
        hi = x[half:, :]
        return jnp.concatenate([lo * cs - hi * sn, hi * cs + lo * sn], axis=0).astype(BF16)

    def turned(x, sn):
        return turned_by(x, cosine, sn)

    loads[0].wait()
    loads[1].wait()
    own_t = turned(k_ref[...].T.astype(F32), sine)
    kt_all[place] = own_t
    kv_all[place, 0] = own_t.T
    pl.semaphore_wait(barrier, 12)

    def kv_copy(q):
        return rc(kv_all.at[place], kv_all.at[place], kv_s.at[q], kv_r.at[place], at_place(q))

    @pl.when(core == 0)
    def _():
        kv_copy(place + 1).start()

    def kv_start(i, carry):
        kv_copy(2 * i + core).start()
        return carry

    lax.fori_loop(chip + 1, QUAD, kv_start, 0)
    z_tell(0)
    x_tell(0)

    loads[2].wait()
    loads[3].wait()
    for i in range(heads):
        cols = slice(i * HEAD_SIZE, (i + 1) * HEAD_SIZE)
        span = slice(i * rows, (i + 1) * rows)
        q_rot[span, :] = turned(q_ref[:, cols].T.astype(F32), sine).T
        do_hm[span, :] = do_ref[:, cols]

    def head_loop(fn):
        lax.fori_loop(1, head_count, lambda i, c: (fn((h + i) % head_count), c)[1], 0)

    def forward_block(j, masked):
        keys = kv_all[j, 0]
        values = kv_all[j, 1]
        if not masked:
            kt_all[j] = keys.T
        for i in range(heads):
            span = slice(i * rows, (i + 1) * rows)
            if i % WIDE == 0:
                part = slice(i * rows, (i + WIDE) * rows)
                st_wide = dot_nt(keys, q_rot[part, :])
                dp_wide = dot_nt(values, do_hm[part, :])
            here = slice((i % WIDE) * rows, (i % WIDE + 1) * rows)
            st = st_wide[:, here]
            dp = dp_wide[:, here]
            if masked:
                key_pos = lax.broadcasted_iota(jnp.int32, (rows, rows), 0)
                query_pos = lax.broadcasted_iota(jnp.int32, (rows, rows), 1)
                st = jnp.where(key_pos <= query_pos, st, -1e30)
                top = jnp.max(st, axis=0, keepdims=True)
                e = jnp.exp2((st - top) * (score_scale * LOG2E))
                l_run[i] = jnp.sum(e, axis=0, keepdims=True)
                d_run[i] = jnp.sum(e * dp, axis=0, keepdims=True)
            else:
                old = m_run[i]
                top = jnp.maximum(old, jnp.max(st, axis=0, keepdims=True))
                e = jnp.exp2((st - top) * (score_scale * LOG2E))
                fix = jnp.exp2((old - top) * (score_scale * LOG2E))
                l_run[i] = l_run[i] * fix + jnp.sum(e, axis=0, keepdims=True)
                d_run[i] = d_run[i] * fix + jnp.sum(e * dp, axis=0, keepdims=True)
            m_run[i] = top
            m_blk[j, i] = top
            e_buf[j, :, span] = e
            dp_buf[j, :, span] = dp

    forward_block(place, True)
    pl.semaphore_wait(x_hop.at[0], 2)
    x_tell(1)
    pl.semaphore_wait(z_hop.at[0], 2)
    z_tell(1)

    def table_step(i, carry):
        away = (s + seq_count - place + 2 * i + core) % seq_count - s
        turn = frequency * (away * rows).astype(F32)
        cs = jnp.cos(turn)
        sn = jnp.sin(turn)
        table[i, 0] = cosine * cs - sine * sn
        table[i, 1] = sine * cs + cosine * sn
        return carry

    lax.fori_loop(0, chip, table_step, 0)

    def kv_arrived(j):
        rc(kv_all.at[j], kv_all.at[j], kv_s.at[j], kv_r.at[j], partner).wait_recv()

    def relay(j):
        kv_arrived(j)
        rc(kv_all.at[j], kv_all.at[j], fw_s.at[j], kv_r.at[j], partner).start()

    @pl.when(core == 1)
    def _():
        kv_arrived(place - 1)
        forward_block(place - 1, False)

    @pl.when(chip > 0)
    def _():
        relay(place - 2)

    def forward_step(n, carry):
        i = n // 2
        par = n % 2
        base = 2 * (chip - 1 - i)

        @pl.when(par == 1)
        def _():
            @pl.when(i < chip - 1)
            def _():
                relay(base - 2 + core)

            kv_arrived(base + 1 - core)

        forward_block(base + core + par * (1 - 2 * core), False)
        return carry

    lax.fori_loop(0, 2 * chip, forward_step, 0)

    pl.semaphore_wait(x_hop.at[1], 2)
    pl.semaphore_wait(z_hop.at[1], 2)
    z_tell(2)
    for load in loads[4:]:
        load.wait()
    down_out[...] = dot_nt(wd_ref[...], x_ref[...]).astype(BF16)
    down_in[h] = down_out[...]
    head_loop(lambda i: rc(down_out, down_in.at[h], down_s.at[i], down_r.at[h], at_head(i)).start())

    for i in range(heads):
        inv = 1.0 / l_run[i]
        l_run[i] = inv
        d_run[i] = d_run[i] * inv

    dq_t[...] = jnp.zeros_like(dq_t)

    def backward_block(j):
        for i in range(heads):
            span = slice(i * rows, (i + 1) * rows)
            scale = jnp.exp2((m_blk[j, i] - m_run[i]) * (score_scale * LOG2E)) * l_run[i]
            prob = e_buf[j, :, span] * scale
            p_t[:, span] = prob.astype(BF16)
            ds_t[:, span] = (prob * (dp_buf[j, :, span] - d_run[i])).astype(BF16)
            if i % 4 == 3:
                part = slice((i - 3) * rows, (i + 1) * rows)
                key_new = dot(ds_t[:, part], q_rot[part, :])
                value_new = dot(p_t[:, part], do_hm[part, :])
                key_part = key_new if i == 3 else key_part + key_new
                value_part = value_new if i == 3 else value_part + value_new
        dq_t[...] += dot(kt_all[j], ds_t[...])
        return key_part, value_part

    def part_copy_pair(j):
        return rc(part_out.at[j], pair_in.at[j], part_s.at[j], pair_r.at[j], partner)

    def part_copy_chip(j):
        return rc(part_out.at[j], chip_in.at[chip], part_s.at[j], chip_r.at[chip], at_place(j))

    def back_rows(key_sum, value_sum, cs, sn):
        key_back = turned_by(key_sum.T * score_scale, cs, -sn)
        return jnp.concatenate(
            [dot(ukv_ref[0:8, :], key_back), dot_nt(ukv_ref[8:16, :], value_sum)], axis=0
        )

    def mini_copy(i):
        return rc(mini_out.at[i], mini_in.at[chip], mini_s.at[i], mini_r.at[chip], at_place(2 * i + core))

    def backward_step(w, carry):
        par = w % 2
        j = 2 * (w // 2) + (1 - core) + par * (2 * core - 1)
        key_part, value_part = backward_block(j)

        @pl.when(par == 0)
        def _():
            part_out[j, 0] = key_part.astype(BF16)
            part_out[j, 1] = value_part.astype(BF16)
            part_copy_pair(j).start()

        @pl.when(par == 1)
        def _():
            part_copy_pair(j).wait_recv()
            key_sum = key_part + pair_in[j, 0].astype(F32)
            value_sum = (value_part + pair_in[j, 1].astype(F32)).astype(BF16)
            i = w // 2
            mini_out[i] = back_rows(key_sum, value_sum, table[i, 0], table[i, 1]).astype(BF16)
            mini_copy(i).start()
            part_out[j, 0] = key_sum.astype(BF16)
            part_out[j, 1] = value_sum
            part_copy_chip(j).start()

        return carry

    lax.fori_loop(0, place, backward_step, 0)
    key_part, value_part = backward_block(place)
    acc[0] = key_part
    acc[1] = value_part

    pl.semaphore_wait(z_hop.at[2], 2)

    for i in range(heads):
        span = slice(i * rows, (i + 1) * rows)
        cols = slice(i * HEAD_SIZE, (i + 1) * HEAD_SIZE)
        grad = turned(dq_t[:, span] * score_scale, -sine)
        dqt_b[cols, :] = grad
        dq_ref[:, cols] = grad.T
    back_out[0:8, :] = dot(uq_ref[...], dqt_b[...]).astype(BF16)

    @pl.when(core == 0)
    def _():
        rc(part_out.at[place], pair_in.at[place], part_s.at[place], pair_r.at[place], partner).wait_recv()
        acc[...] += pair_in[place].astype(F32)

    back_kv[...] = back_rows(acc[0], acc[1].astype(BF16), cosine, sine)

    def mini_add(i, carry):
        rc(mini_out.at[0], mini_in.at[i], mini_s.at[0], mini_r.at[i], at_place(2 * i + core)).wait_recv()
        back_kv[...] += mini_in[i].astype(F32)
        return carry

    lax.fori_loop(chip + 1, QUAD, mini_add, 0)
    back_out[8:24, :] = back_kv[...].astype(BF16)
    back_in[h] = back_out[...]
    head_loop(lambda i: rc(back_out, back_in.at[h], back_s.at[i], back_r.at[h], at_head(i)).start())

    def chip_add(i, carry):
        rc(part_out.at[place], chip_in.at[i], part_s.at[place], chip_r.at[i], at_place(2 * i + core)).wait_recv()
        acc[...] += chip_in[i].astype(F32)
        return carry

    lax.fori_loop(chip + 1, QUAD, chip_add, 0)
    dk_ref[...] = turned(acc[0].T * score_scale, -sine).T
    dv_ref[...] = acc[1].astype(BF16)

    def summed(ref, count):
        total = ref[0].astype(F32)
        for i in range(1, count):
            total = total + ref[i].astype(F32)
        return total

    def unit_loop(fn):
        for i in range(1, QUAD):
            fn((unit + i) % QUAD)

    def z_loop(fn):
        lax.fori_loop(1, z_count, lambda i, c: (fn((z + i) % z_count), c)[1], 0)

    class Reduce:
        def __init__(self, ro, ri, zo, zi, go, gi, rss, rsr, zs, zr, gs, gr):
            self.refs = (ro, ri, zo, zi, go, gi)
            self.rs = lambda i: rc(ro.at[i], ri.at[unit], rss.at[i], rsr.at[unit], at_unit(i))
            self.rw = lambda i: rc(ro.at[i], ri.at[i], rss.at[i], rsr.at[i], at_unit(i))
            self.zs = lambda i: rc(zo, zi.at[z], zs.at[i], zr.at[z], at_z(i))
            self.zw = lambda i: rc(zo, zi.at[i], zs.at[i], zr.at[i], at_z(i))
            self.gs = lambda i: rc(go, gi.at[unit], gs.at[i], gr.at[unit], at_unit(i))
            self.gw = lambda i: rc(go, gi.at[i], gs.at[i], gr.at[i], at_unit(i))

        def scatter(self):
            ro, ri = self.refs[:2]
            unit_loop(lambda i: self.rs(i).start())
            ri[unit] = ro[unit]

        def across(self):
            ro, ri, zo, zi = self.refs[:4]
            unit_loop(lambda i: self.rw(i).wait_recv())
            zo[...] = summed(ri, QUAD).astype(BF16)
            z_loop(lambda i: self.zs(i).start())
            zi[z] = zo[...]

        def gather(self):
            zi, go, gi = self.refs[3:]
            z_loop(lambda i: self.zw(i).wait_recv())
            go[...] = summed(zi, z_count).astype(BF16)
            unit_loop(lambda i: self.gs(i).start())
            gi[unit] = go[...]

        def finish(self):
            unit_loop(lambda i: self.gw(i).wait_recv())

        def drain(self):
            unit_loop(lambda i: self.rw(i).wait_send())
            z_loop(lambda i: self.zw(i).wait_send())
            unit_loop(lambda i: self.gw(i).wait_send())

    first = Reduce(rs1_out, rs1_in, z1_out, z1_in, g1_out, g1_in, rs1_s, rs1_r, z1_s, z1_r, g1_s, g1_r)
    second = Reduce(rs2_out, rs2_in, z2_out, z2_in, g2_out, g2_in, rs2_s, rs2_r, z2_s, z2_r, g2_s, g2_r)


    head_loop(lambda i: rc(down_out, down_in.at[i], down_s.at[i], down_r.at[i], at_head(i)).wait_recv())
    down_act = summed(down_in, head_count).astype(BF16)
    up_query = (2.0 * dot(down_act[0:8, :], dq_ref[...])).astype(BF16)
    up_key = (2.0 * dot(down_act[8:16, :], dk_ref[...])).astype(BF16)
    up_value = (2.0 * dot(down_act[16:24, :], dv_ref[...])).astype(BF16)
    chunk = width // QUAD
    for i in range(QUAD):
        rs1_out[i, 0:8, :] = up_query[:, i * chunk : (i + 1) * chunk]
        rs1_out[i, 8:16, 0:HEAD_SIZE] = up_key
        rs1_out[i, 8:16, HEAD_SIZE:] = up_value
    first.scatter()
    first.across()

    head_loop(lambda i: rc(back_out, back_in.at[i], back_s.at[i], back_r.at[i], at_head(i)).wait_recv())
    back_act = summed(back_in, head_count).astype(BF16)
    down_grad = (2.0 * dot(back_act, x_ref[...])).astype(BF16)
    for i in range(QUAD):
        rs2_out[i] = down_grad[:, i * chunk : (i + 1) * chunk]
    second.scatter()
    second.across()
    first.gather()
    second.gather()
    first.finish()
    for i in range(QUAD):
        guq_ref[:, i * chunk : (i + 1) * chunk] = g1_in[i, 0:8, :].astype(F32)
    gukv_ref[0:8, :] = g1_out[8:16, 0:HEAD_SIZE].astype(F32)
    gukv_ref[8:16, :] = g1_out[8:16, HEAD_SIZE:].astype(F32)
    second.finish()
    for i in range(QUAD):
        gd_ref[:, i * chunk : (i + 1) * chunk] = g2_in[i].astype(F32)

    @pl.when(core == 0)
    def _():
        kv_copy(place + 1).wait_send()

    lax.fori_loop(chip + 1, QUAD, lambda i, c: (kv_copy(2 * i + core).wait_send(), c)[1], 0)

    def drain_block(i, carry):
        j = 2 * i + core
        rc(kv_all.at[j], kv_all.at[j], fw_s.at[j], kv_r.at[j], partner).wait_send()
        return carry

    lax.fori_loop(0, chip, drain_block, 0)
    lax.fori_loop(0, chip, lambda i, c: (mini_copy(i).wait_send(), c)[1], 0)
    lax.fori_loop(0, place, lambda j, c: (part_copy_pair(j).wait_send(), c)[1], 0)
    head_loop(lambda i: rc(down_out, down_in.at[i], down_s.at[i], down_r.at[i], at_head(i)).wait_send())
    head_loop(lambda i: rc(back_out, back_in.at[i], back_s.at[i], back_r.at[i], at_head(i)).wait_send())
    first.drain()
    second.drain()


def hand_over(*refs):
    copies = [pltpu.make_async_copy(refs[i], refs[6 + i], refs[12].at[i]) for i in range(6)]
    for copy in copies:
        copy.start()
    for copy in copies:
        copy.wait()


def body(x, q, k, v, do, wd, uq, ukv):
    rows, width = q.shape
    seq_count = lax.axis_size("seq")
    head_count = lax.axis_size("head")
    heads = width // HEAD_SIZE
    features = x.shape[1]
    chunk = width // QUAD
    z_count = seq_count // QUAD
    vmem = pl.BlockSpec(memory_space=pltpu.VMEM)
    hbm = pl.BlockSpec(memory_space=pl.ANY)
    dma = pltpu.SemaphoreType.DMA
    reduce_bufs = []
    for depth in (16, 24):
        reduce_bufs += [
            pltpu.VMEM((QUAD, depth, chunk), BF16),
            pltpu.VMEM((QUAD, depth, chunk), BF16),
            pltpu.VMEM((depth, chunk), BF16),
            pltpu.VMEM((z_count, depth, chunk), BF16),
            pltpu.VMEM((depth, chunk), BF16),
            pltpu.VMEM((QUAD, depth, chunk), BF16),
        ]
    reduce_sems = [dma((n,)) for n in (QUAD, QUAD, z_count, z_count, QUAD, QUAD)] * 2
    outs = pl.pallas_call(
        functools.partial(kernel, seq_count, head_count),
        out_shape=(
            pltpu.VMEM((rows, width), BF16),
            pltpu.VMEM((rows, HEAD_SIZE), BF16),
            pltpu.VMEM((rows, HEAD_SIZE), BF16),
            pltpu.VMEM((24, features), F32),
            pltpu.VMEM((8, width), F32),
            pltpu.VMEM((16, HEAD_SIZE), F32),
        ),
        in_specs=[hbm] * 8,
        out_specs=(vmem,) * 6,
        scratch_shapes=[
            pltpu.VMEM((rows, width), BF16),
            pltpu.VMEM((rows, HEAD_SIZE), BF16),
            pltpu.VMEM((rows, width), BF16),
            pltpu.VMEM((rows, features), BF16),
            pltpu.VMEM((24, features), BF16),
            pltpu.VMEM((8, width), BF16),
            pltpu.VMEM((16, HEAD_SIZE), BF16),
            pltpu.VMEM((GROUP, 2, rows, HEAD_SIZE), BF16),
            pltpu.VMEM((GROUP, HEAD_SIZE, rows), BF16),
            pltpu.VMEM((heads * rows, HEAD_SIZE), BF16),
            pltpu.VMEM((heads * rows, HEAD_SIZE), BF16),
            pltpu.VMEM((width, rows), BF16),
            pltpu.VMEM((GROUP, rows, heads * rows), F32),
            pltpu.VMEM((GROUP, rows, heads * rows), F32),
            pltpu.VMEM((GROUP, heads, 1, rows), F32),
            pltpu.VMEM((heads, 1, rows), F32),
            pltpu.VMEM((heads, 1, rows), F32),
            pltpu.VMEM((heads, 1, rows), F32),
            pltpu.VMEM((rows, heads * rows), BF16),
            pltpu.VMEM((rows, heads * rows), BF16),
            pltpu.VMEM((HEAD_SIZE, heads * rows), F32),
            pltpu.VMEM((2, rows, HEAD_SIZE), F32),
            pltpu.VMEM((GROUP, 2, rows, HEAD_SIZE), BF16),
            pltpu.VMEM((GROUP, 2, rows, HEAD_SIZE), BF16),
            pltpu.VMEM((QUAD, 2, rows, HEAD_SIZE), BF16),
            pltpu.VMEM((QUAD, 2, HEAD_SIZE // 2, rows), F32),
            pltpu.VMEM((QUAD, 16, rows), BF16),
            pltpu.VMEM((QUAD, 16, rows), BF16),
            pltpu.VMEM((16, rows), F32),
            pltpu.VMEM((24, rows), BF16),
            pltpu.VMEM((head_count, 24, rows), BF16),
            pltpu.VMEM((24, rows), BF16),
            pltpu.VMEM((head_count, 24, rows), BF16),
        ]
        + reduce_bufs
        + [pltpu.SemaphoreType.REGULAR((3,)), pltpu.SemaphoreType.REGULAR((2,))]
        + [dma((8,))]
        + [dma((GROUP,))] * 5
        + [dma((QUAD,))] * 3
        + [dma((head_count,))] * 4
        + reduce_sems,
        compiler_params=pltpu.CompilerParams(
            collective_id=0, has_side_effects=True, vmem_limit_bytes=54 * 1024 * 1024
        ),
    )(
        q,
        k,
        v,
        do,
        x,
        wd.reshape(24, features),
        uq,
        ukv.reshape(16, HEAD_SIZE),
    )
    dq, dk, dv, gd, guq, gukv = pl.pallas_call(
        hand_over,
        out_shape=tuple(jax.ShapeDtypeStruct(o.shape, o.dtype) for o in outs),
        in_specs=[vmem] * 6,
        out_specs=(hbm,) * 6,
        scratch_shapes=[dma((6,))],
    )(*[pltpu.with_memory_space_constraint(o, pltpu.VMEM) for o in outs])
    return (dq, dk, dv, gd.reshape(3, 8, features), guq, gukv.reshape(2, 8, HEAD_SIZE))


def solution(mesh):
    tokens = P("seq", "head")
    return jax.shard_map(
        body,
        mesh=mesh,
        in_specs=(tokens,) * 5 + (P(None, None, "head"), P(None, "head"), P(None, None, "head")),
        out_specs=(tokens,) * 3 + (P(None, None, "head"), P(None, "head"), P(None, None, "head")),
        check_vma=False,
    )
```

```python
import functools

import jax
import jax.numpy as jnp
from jax import lax
from jax.experimental import pallas as pl
from jax.experimental.pallas import tpu as pltpu
from jax.sharding import PartitionSpec as P

HEAD_SIZE = 128
POSITION_SCALE = 0.04096
LOG2E = 1.4426950408889634
MESH = pl.DeviceIdType.MESH
F32 = jnp.float32
BF16 = jnp.bfloat16
GROUP = 8
QUAD = 4
WIDE = 2
NT = (((1,), (1,)), ((), ()))


def dot(a, b):
    return jnp.dot(a, b, preferred_element_type=F32)


def dot_nt(a, b):
    return lax.dot_general(a, b, NT, preferred_element_type=F32)


def kernel(
    seq_count,
    head_count,
    q_hbm,
    k_hbm,
    v_hbm,
    do_hbm,
    x_hbm,
    wd_hbm,
    uq_hbm,
    ukv_hbm,
    dq_ref,
    dk_ref,
    dv_ref,
    gd_ref,
    guq_ref,
    gukv_ref,
    q_ref,
    k_ref,
    do_ref,
    x_ref,
    wd_ref,
    uq_ref,
    ukv_ref,
    kv_all,
    kt_all,
    q_rot,
    do_hm,
    dqt_b,
    e_buf,
    dp_buf,
    m_blk,
    m_run,
    l_run,
    d_run,
    p_t,
    ds_t,
    dq_t,
    acc,
    part_out,
    pair_in,
    chip_in,
    table,
    mini_out,
    mini_in,
    back_kv,
    down_out,
    down_in,
    back_out,
    back_in,
    rs1_out,
    rs1_in,
    z1_out,
    z1_in,
    g1_out,
    g1_in,
    rs2_out,
    rs2_in,
    z2_out,
    z2_in,
    g2_out,
    g2_in,
    z_hop,
    x_hop,
    in_s,
    kv_s,
    kv_r,
    fw_s,
    part_s,
    pair_r,
    chip_r,
    mini_s,
    mini_r,
    down_s,
    down_r,
    back_s,
    back_r,
    rs1_s,
    rs1_r,
    z1_s,
    z1_r,
    g1_s,
    g1_r,
    rs2_s,
    rs2_r,
    z2_s,
    z2_r,
    g2_s,
    g2_r,
):
    rows = k_ref.shape[0]
    heads = q_ref.shape[1] // HEAD_SIZE
    width = heads * HEAD_SIZE
    score_scale = HEAD_SIZE ** -0.5
    s = lax.axis_index("seq")
    h = lax.axis_index("head")
    shift = jnp.where(h >= head_count // 2, GROUP // 2, 0)
    place = (s + seq_count - shift) % GROUP
    chip = place // 2
    core = place % 2
    unit = s % QUAD
    z = s // QUAD
    z_count = seq_count // QUAD

    def at_place(q):
        return ((s + seq_count - place + q) % seq_count, h)

    partner = at_place(place + 1 - 2 * core)

    def at_head(i):
        return (s, i)

    def at_unit(i):
        return (z * QUAD + i, h)

    def at_z(i):
        return (i * QUAD + unit, h)

    def rc(src, dst, ss, rs, dev):
        return pltpu.make_async_remote_copy(
            src_ref=src, dst_ref=dst, send_sem=ss, recv_sem=rs, device_id=dev, device_id_type=MESH
        )

    barrier = pltpu.get_barrier_semaphore()

    def signal(sem, dev):
        pl.semaphore_signal(sem, inc=1, device_id=dev, device_id_type=MESH)

    x_count = head_count // 2
    x_base = h - h % x_count
    z_near = (at_z((z + 1) % z_count), at_z((z + z_count - 1) % z_count))
    x_near = (
        at_head(x_base + (h + 1) % x_count),
        at_head(x_base + (h + x_count - 1) % x_count),
    )

    lax.fori_loop(1, GROUP, lambda i, c: (signal(barrier, at_place((place + i) % GROUP)), c)[1], 0)
    for dev in z_near + x_near + (at_head((h + x_count) % head_count),):
        signal(barrier, dev)

    def z_tell(n):
        for dev in z_near:
            signal(z_hop.at[n], dev)

    def x_tell(n):
        for dev in x_near:
            signal(x_hop.at[n], dev)

    loads = [
        pltpu.make_async_copy(src, dst, in_s.at[i])
        for i, (src, dst) in enumerate(
            (
                (k_hbm, k_ref),
                (v_hbm, kv_all.at[place, 1]),
                (q_hbm, q_ref),
                (do_hbm, do_ref),
                (x_hbm, x_ref),
                (wd_hbm, wd_ref),
                (uq_hbm, uq_ref),
                (ukv_hbm, ukv_ref),
            )
        )
    ]
    for load in loads:
        load.start()

    half = HEAD_SIZE // 2
    feature = lax.broadcasted_iota(jnp.int32, (half, 1), 0).astype(F32)
    frequency = POSITION_SCALE * jnp.exp(feature * (-2.0 / HEAD_SIZE * 9.210340371976184))
    position = (s * rows + lax.broadcasted_iota(jnp.int32, (1, rows), 1)).astype(F32)
    angle = frequency * position
    cosine = jnp.cos(angle)
    sine = jnp.sin(angle)

    def turned_by(x, cs, sn):
        lo = x[:half, :]
        hi = x[half:, :]
        return jnp.concatenate([lo * cs - hi * sn, hi * cs + lo * sn], axis=0).astype(BF16)

    def turned(x, sn):
        return turned_by(x, cosine, sn)

    loads[0].wait()
    loads[1].wait()
    own_t = turned(k_ref[...].T.astype(F32), sine)
    kt_all[place] = own_t
    kv_all[place, 0] = own_t.T
    pl.semaphore_wait(barrier, 12)

    def kv_copy(q):
        return rc(kv_all.at[place], kv_all.at[place], kv_s.at[q], kv_r.at[place], at_place(q))

    @pl.when(core == 0)
    def _():
        kv_copy(place + 1).start()

    def kv_start(i, carry):
        kv_copy(2 * i + core).start()
        return carry

    lax.fori_loop(chip + 1, QUAD, kv_start, 0)
    z_tell(0)
    x_tell(0)

    loads[2].wait()
    loads[3].wait()
    for i in range(heads):
        cols = slice(i * HEAD_SIZE, (i + 1) * HEAD_SIZE)
        span = slice(i * rows, (i + 1) * rows)
        q_rot[span, :] = turned(q_ref[:, cols].T.astype(F32), sine).T
        do_hm[span, :] = do_ref[:, cols]

    def head_loop(fn):
        lax.fori_loop(1, head_count, lambda i, c: (fn((h + i) % head_count), c)[1], 0)

    def forward_block(j, masked):
        keys = kv_all[j, 0]
        values = kv_all[j, 1]
        if not masked:
            kt_all[j] = keys.T
        for i in range(heads):
            span = slice(i * rows, (i + 1) * rows)
            if i % WIDE == 0:
                part = slice(i * rows, (i + WIDE) * rows)
                st_wide = dot_nt(keys, q_rot[part, :])
                dp_wide = dot_nt(values, do_hm[part, :])
            here = slice((i % WIDE) * rows, (i % WIDE + 1) * rows)
            st = st_wide[:, here]
            dp = dp_wide[:, here]
            if masked:
                key_pos = lax.broadcasted_iota(jnp.int32, (rows, rows), 0)
                query_pos = lax.broadcasted_iota(jnp.int32, (rows, rows), 1)
                st = jnp.where(key_pos <= query_pos, st, -1e30)
                top = jnp.max(st, axis=0, keepdims=True)
                e = jnp.exp2((st - top) * (score_scale * LOG2E))
                l_run[i] = jnp.sum(e, axis=0, keepdims=True)
                d_run[i] = jnp.sum(e * dp, axis=0, keepdims=True)
            else:
                old = m_run[i]
                top = jnp.maximum(old, jnp.max(st, axis=0, keepdims=True))
                e = jnp.exp2((st - top) * (score_scale * LOG2E))
                fix = jnp.exp2((old - top) * (score_scale * LOG2E))
                l_run[i] = l_run[i] * fix + jnp.sum(e, axis=0, keepdims=True)
                d_run[i] = d_run[i] * fix + jnp.sum(e * dp, axis=0, keepdims=True)
            m_run[i] = top
            m_blk[j, i] = top
            e_buf[j, :, span] = e
            dp_buf[j, :, span] = dp

    forward_block(place, True)
    pl.semaphore_wait(x_hop.at[0], 2)
    x_tell(1)
    pl.semaphore_wait(z_hop.at[0], 2)
    z_tell(1)

    def kv_arrived(j):
        rc(kv_all.at[j], kv_all.at[j], kv_s.at[j], kv_r.at[j], partner).wait_recv()

    def relay(j):
        kv_arrived(j)
        rc(kv_all.at[j], kv_all.at[j], fw_s.at[j], kv_r.at[j], partner).start()

    @pl.when(core == 1)
    def _():
        kv_arrived(place - 1)
        forward_block(place - 1, False)

    @pl.when(chip > 0)
    def _():
        away = (s + seq_count - 2) % seq_count - s
        turn = frequency * (away * rows).astype(F32)
        cs = jnp.cos(turn)
        sn = jnp.sin(turn)
        table[0] = cosine * cs - sine * sn
        table[1] = sine * cs + cosine * sn

    @pl.when(chip > 0)
    def _():
        relay(place - 2)

    def forward_step(n, carry):
        i = n // 2
        par = n % 2
        base = 2 * (chip - 1 - i)

        @pl.when(par == 1)
        def _():
            @pl.when(i < chip - 1)
            def _():
                relay(base - 2 + core)

            kv_arrived(base + 1 - core)

        forward_block(base + core + par * (1 - 2 * core), False)
        return carry

    lax.fori_loop(0, 2 * chip, forward_step, 0)

    pl.semaphore_wait(x_hop.at[1], 2)
    pl.semaphore_wait(z_hop.at[1], 2)
    z_tell(2)
    for load in loads[4:]:
        load.wait()
    down_out[...] = dot_nt(wd_ref[...], x_ref[...]).astype(BF16)
    down_in[h] = down_out[...]
    head_loop(lambda i: rc(down_out, down_in.at[h], down_s.at[i], down_r.at[h], at_head(i)).start())

    for i in range(heads):
        inv = 1.0 / l_run[i]
        l_run[i] = inv
        d_run[i] = d_run[i] * inv

    dq_t[...] = jnp.zeros_like(dq_t)

    def backward_block(j):
        for i in range(heads):
            span = slice(i * rows, (i + 1) * rows)
            scale = jnp.exp2((m_blk[j, i] - m_run[i]) * (score_scale * LOG2E)) * l_run[i]
            prob = e_buf[j, :, span] * scale
            p_t[:, span] = prob.astype(BF16)
            ds_t[:, span] = (prob * (dp_buf[j, :, span] - d_run[i])).astype(BF16)
            if i % 4 == 3:
                part = slice((i - 3) * rows, (i + 1) * rows)
                key_new = dot(ds_t[:, part], q_rot[part, :])
                value_new = dot(p_t[:, part], do_hm[part, :])
                key_part = key_new if i == 3 else key_part + key_new
                value_part = value_new if i == 3 else value_part + value_new
        dq_t[...] += dot(kt_all[j], ds_t[...])
        return key_part, value_part

    def part_copy_pair(j):
        return rc(part_out.at[j], pair_in.at[j], part_s.at[j], pair_r.at[j], partner)

    def part_copy_chip(j):
        return rc(part_out.at[j], chip_in.at[chip], part_s.at[j], chip_r.at[chip], at_place(j))

    def back_rows(key_sum, value_sum, cs, sn):
        key_back = turned_by(key_sum.T * score_scale, cs, -sn)
        return jnp.concatenate(
            [dot(ukv_ref[0:8, :], key_back), dot_nt(ukv_ref[8:16, :], value_sum)], axis=0
        )

    def mini_copy(q):
        return rc(mini_out, mini_in, mini_s.at[0], mini_r.at[0], at_place(q))

    def backward_step(w, carry):
        par = w % 2
        j = 2 * (w // 2) + (1 - core) + par * (2 * core - 1)
        key_part, value_part = backward_block(j)

        @pl.when(par == 0)
        def _():
            part_out[j, 0] = key_part.astype(BF16)
            part_out[j, 1] = value_part.astype(BF16)
            part_copy_pair(j).start()

        @pl.when(par == 1)
        def _():
            part_copy_pair(j).wait_recv()
            key_sum = key_part + pair_in[j, 0].astype(F32)
            value_sum = (value_part + pair_in[j, 1].astype(F32)).astype(BF16)

            @pl.when(w // 2 == chip - 1)
            def _():
                mini_out[...] = back_rows(key_sum, value_sum, table[0], table[1]).astype(BF16)
                mini_copy(place - 2).start()

            part_out[j, 0] = key_sum.astype(BF16)
            part_out[j, 1] = value_sum
            part_copy_chip(j).start()

        return carry

    lax.fori_loop(0, place, backward_step, 0)
    key_part, value_part = backward_block(place)
    acc[0] = key_part
    acc[1] = value_part

    pl.semaphore_wait(z_hop.at[2], 2)

    for i in range(heads):
        span = slice(i * rows, (i + 1) * rows)
        cols = slice(i * HEAD_SIZE, (i + 1) * HEAD_SIZE)
        grad = turned(dq_t[:, span] * score_scale, -sine)
        dqt_b[cols, :] = grad
        dq_ref[:, cols] = grad.T
    back_out[0:8, :] = dot(uq_ref[...], dqt_b[...]).astype(BF16)

    @pl.when(core == 0)
    def _():
        rc(part_out.at[place], pair_in.at[place], part_s.at[place], pair_r.at[place], partner).wait_recv()
        acc[...] += pair_in[place].astype(F32)

    def chip_add(i, carry):
        rc(part_out.at[place], chip_in.at[i], part_s.at[place], chip_r.at[i], at_place(2 * i + core)).wait_recv()
        acc[...] += chip_in[i].astype(F32)
        return carry

    lax.fori_loop(chip + 2, QUAD, chip_add, 0)
    back_kv[...] = back_rows(acc[0], acc[1].astype(BF16), cosine, sine)

    @pl.when(chip < QUAD - 1)
    def _():
        mini_copy(place + 2).wait_recv()
        back_kv[...] += mini_in[...].astype(F32)

    back_out[8:24, :] = back_kv[...].astype(BF16)
    back_in[h] = back_out[...]
    head_loop(lambda i: rc(back_out, back_in.at[h], back_s.at[i], back_r.at[h], at_head(i)).start())

    @pl.when(chip < QUAD - 1)
    def _():
        chip_add(chip + 1, 0)

    dk_ref[...] = turned(acc[0].T * score_scale, -sine).T
    dv_ref[...] = acc[1].astype(BF16)

    def summed(ref, count):
        total = ref[0].astype(F32)
        for i in range(1, count):
            total = total + ref[i].astype(F32)
        return total

    def unit_loop(fn):
        for i in range(1, QUAD):
            fn((unit + i) % QUAD)

    def z_loop(fn):
        lax.fori_loop(1, z_count, lambda i, c: (fn((z + i) % z_count), c)[1], 0)

    class Reduce:
        def __init__(self, ro, ri, zo, zi, go, gi, rss, rsr, zs, zr, gs, gr):
            self.refs = (ro, ri, zo, zi, go, gi)
            self.rs = lambda i: rc(ro.at[i], ri.at[unit], rss.at[i], rsr.at[unit], at_unit(i))
            self.rw = lambda i: rc(ro.at[i], ri.at[i], rss.at[i], rsr.at[i], at_unit(i))
            self.zs = lambda i: rc(zo, zi.at[z], zs.at[i], zr.at[z], at_z(i))
            self.zw = lambda i: rc(zo, zi.at[i], zs.at[i], zr.at[i], at_z(i))
            self.gs = lambda i: rc(go, gi.at[unit], gs.at[i], gr.at[unit], at_unit(i))
            self.gw = lambda i: rc(go, gi.at[i], gs.at[i], gr.at[i], at_unit(i))

        def scatter(self):
            ro, ri = self.refs[:2]
            unit_loop(lambda i: self.rs(i).start())
            ri[unit] = ro[unit]

        def across(self):
            ro, ri, zo, zi = self.refs[:4]
            unit_loop(lambda i: self.rw(i).wait_recv())
            zo[...] = summed(ri, QUAD).astype(BF16)
            z_loop(lambda i: self.zs(i).start())
            zi[z] = zo[...]

        def gather(self):
            zi, go, gi = self.refs[3:]
            z_loop(lambda i: self.zw(i).wait_recv())
            go[...] = summed(zi, z_count).astype(BF16)
            unit_loop(lambda i: self.gs(i).start())
            gi[unit] = go[...]

        def finish(self):
            unit_loop(lambda i: self.gw(i).wait_recv())

        def drain(self):
            unit_loop(lambda i: self.rw(i).wait_send())
            z_loop(lambda i: self.zw(i).wait_send())
            unit_loop(lambda i: self.gw(i).wait_send())

    first = Reduce(rs1_out, rs1_in, z1_out, z1_in, g1_out, g1_in, rs1_s, rs1_r, z1_s, z1_r, g1_s, g1_r)
    second = Reduce(rs2_out, rs2_in, z2_out, z2_in, g2_out, g2_in, rs2_s, rs2_r, z2_s, z2_r, g2_s, g2_r)


    head_loop(lambda i: rc(down_out, down_in.at[i], down_s.at[i], down_r.at[i], at_head(i)).wait_recv())
    down_act = summed(down_in, head_count).astype(BF16)
    up_query = (2.0 * dot(down_act[0:8, :], dq_ref[...])).astype(BF16)
    up_key = (2.0 * dot(down_act[8:16, :], dk_ref[...])).astype(BF16)
    up_value = (2.0 * dot(down_act[16:24, :], dv_ref[...])).astype(BF16)
    chunk = width // QUAD
    for i in range(QUAD):
        rs1_out[i, 0:8, :] = up_query[:, i * chunk : (i + 1) * chunk]
        rs1_out[i, 8:16, 0:HEAD_SIZE] = up_key
        rs1_out[i, 8:16, HEAD_SIZE:] = up_value
    first.scatter()

    head_loop(lambda i: rc(back_out, back_in.at[i], back_s.at[i], back_r.at[i], at_head(i)).wait_recv())
    back_act = summed(back_in, head_count).astype(BF16)
    down_grad = (2.0 * dot(back_act, x_ref[...])).astype(BF16)
    for i in range(QUAD):
        rs2_out[i] = down_grad[:, i * chunk : (i + 1) * chunk]
    second.scatter()
    first.across()
    second.across()
    first.gather()
    second.gather()
    first.finish()
    for i in range(QUAD):
        guq_ref[:, i * chunk : (i + 1) * chunk] = g1_in[i, 0:8, :].astype(F32)
    gukv_ref[0:8, :] = g1_out[8:16, 0:HEAD_SIZE].astype(F32)
    gukv_ref[8:16, :] = g1_out[8:16, HEAD_SIZE:].astype(F32)
    second.finish()
    for i in range(QUAD):
        gd_ref[:, i * chunk : (i + 1) * chunk] = g2_in[i].astype(F32)

    @pl.when(core == 0)
    def _():
        kv_copy(place + 1).wait_send()

    lax.fori_loop(chip + 1, QUAD, lambda i, c: (kv_copy(2 * i + core).wait_send(), c)[1], 0)

    def drain_block(i, carry):
        j = 2 * i + core
        rc(kv_all.at[j], kv_all.at[j], fw_s.at[j], kv_r.at[j], partner).wait_send()
        return carry

    lax.fori_loop(0, chip, drain_block, 0)

    @pl.when(chip > 0)
    def _():
        mini_copy(place - 2).wait_send()

    lax.fori_loop(0, place, lambda j, c: (part_copy_pair(j).wait_send(), c)[1], 0)
    head_loop(lambda i: rc(down_out, down_in.at[i], down_s.at[i], down_r.at[i], at_head(i)).wait_send())
    head_loop(lambda i: rc(back_out, back_in.at[i], back_s.at[i], back_r.at[i], at_head(i)).wait_send())
    first.drain()
    second.drain()


def hand_over(*refs):
    copies = [pltpu.make_async_copy(refs[i], refs[6 + i], refs[12].at[i]) for i in range(6)]
    for copy in copies:
        copy.start()
    for copy in copies:
        copy.wait()


def body(x, q, k, v, do, wd, uq, ukv):
    rows, width = q.shape
    seq_count = lax.axis_size("seq")
    head_count = lax.axis_size("head")
    heads = width // HEAD_SIZE
    features = x.shape[1]
    chunk = width // QUAD
    z_count = seq_count // QUAD
    vmem = pl.BlockSpec(memory_space=pltpu.VMEM)
    hbm = pl.BlockSpec(memory_space=pl.ANY)
    dma = pltpu.SemaphoreType.DMA
    reduce_bufs = []
    for depth in (16, 24):
        reduce_bufs += [
            pltpu.VMEM((QUAD, depth, chunk), BF16),
            pltpu.VMEM((QUAD, depth, chunk), BF16),
            pltpu.VMEM((depth, chunk), BF16),
            pltpu.VMEM((z_count, depth, chunk), BF16),
            pltpu.VMEM((depth, chunk), BF16),
            pltpu.VMEM((QUAD, depth, chunk), BF16),
        ]
    reduce_sems = [dma((n,)) for n in (QUAD, QUAD, z_count, z_count, QUAD, QUAD)] * 2
    outs = pl.pallas_call(
        functools.partial(kernel, seq_count, head_count),
        out_shape=(
            pltpu.VMEM((rows, width), BF16),
            pltpu.VMEM((rows, HEAD_SIZE), BF16),
            pltpu.VMEM((rows, HEAD_SIZE), BF16),
            pltpu.VMEM((24, features), F32),
            pltpu.VMEM((8, width), F32),
            pltpu.VMEM((16, HEAD_SIZE), F32),
        ),
        in_specs=[hbm] * 8,
        out_specs=(vmem,) * 6,
        scratch_shapes=[
            pltpu.VMEM((rows, width), BF16),
            pltpu.VMEM((rows, HEAD_SIZE), BF16),
            pltpu.VMEM((rows, width), BF16),
            pltpu.VMEM((rows, features), BF16),
            pltpu.VMEM((24, features), BF16),
            pltpu.VMEM((8, width), BF16),
            pltpu.VMEM((16, HEAD_SIZE), BF16),
            pltpu.VMEM((GROUP, 2, rows, HEAD_SIZE), BF16),
            pltpu.VMEM((GROUP, HEAD_SIZE, rows), BF16),
            pltpu.VMEM((heads * rows, HEAD_SIZE), BF16),
            pltpu.VMEM((heads * rows, HEAD_SIZE), BF16),
            pltpu.VMEM((width, rows), BF16),
            pltpu.VMEM((GROUP, rows, heads * rows), F32),
            pltpu.VMEM((GROUP, rows, heads * rows), F32),
            pltpu.VMEM((GROUP, heads, 1, rows), F32),
            pltpu.VMEM((heads, 1, rows), F32),
            pltpu.VMEM((heads, 1, rows), F32),
            pltpu.VMEM((heads, 1, rows), F32),
            pltpu.VMEM((rows, heads * rows), BF16),
            pltpu.VMEM((rows, heads * rows), BF16),
            pltpu.VMEM((HEAD_SIZE, heads * rows), F32),
            pltpu.VMEM((2, rows, HEAD_SIZE), F32),
            pltpu.VMEM((GROUP, 2, rows, HEAD_SIZE), BF16),
            pltpu.VMEM((GROUP, 2, rows, HEAD_SIZE), BF16),
            pltpu.VMEM((QUAD, 2, rows, HEAD_SIZE), BF16),
            pltpu.VMEM((2, HEAD_SIZE // 2, rows), F32),
            pltpu.VMEM((16, rows), BF16),
            pltpu.VMEM((16, rows), BF16),
            pltpu.VMEM((16, rows), F32),
            pltpu.VMEM((24, rows), BF16),
            pltpu.VMEM((head_count, 24, rows), BF16),
            pltpu.VMEM((24, rows), BF16),
            pltpu.VMEM((head_count, 24, rows), BF16),
        ]
        + reduce_bufs
        + [pltpu.SemaphoreType.REGULAR((3,)), pltpu.SemaphoreType.REGULAR((2,))]
        + [dma((8,))]
        + [dma((GROUP,))] * 5
        + [dma((QUAD,)), dma((1,)), dma((1,))]
        + [dma((head_count,))] * 4
        + reduce_sems,
        compiler_params=pltpu.CompilerParams(
            collective_id=0, has_side_effects=True, vmem_limit_bytes=54 * 1024 * 1024
        ),
    )(
        q,
        k,
        v,
        do,
        x,
        wd.reshape(24, features),
        uq,
        ukv.reshape(16, HEAD_SIZE),
    )
    dq, dk, dv, gd, guq, gukv = pl.pallas_call(
        hand_over,
        out_shape=tuple(jax.ShapeDtypeStruct(o.shape, o.dtype) for o in outs),
        in_specs=[vmem] * 6,
        out_specs=(hbm,) * 6,
        scratch_shapes=[dma((6,))],
    )(*[pltpu.with_memory_space_constraint(o, pltpu.VMEM) for o in outs])
    return (dq, dk, dv, gd.reshape(3, 8, features), guq, gukv.reshape(2, 8, HEAD_SIZE))


def solution(mesh):
    tokens = P("seq", "head")
    return jax.shard_map(
        body,
        mesh=mesh,
        in_specs=(tokens,) * 5 + (P(None, None, "head"), P(None, "head"), P(None, None, "head")),
        out_specs=(tokens,) * 3 + (P(None, None, "head"), P(None, "head"), P(None, None, "head")),
        check_vma=False,
    )
```
